128 devices in a mesh: orb: 8 (over x, y_lo), aux: 16 (over z, y_hi, core).
Axes of the slice: x: 4, y: 4 (y_hi: 2, y_lo: 2; y = y_hi * 2 + y_lo), z: 4, core: 2. Of those that a mesh axis runs over, the one named last changes fastest.
Arguments:
- raw_rows: bfloat16 [512, 2048, 128], P('orb', 'aux'), may hold values from -4 to 4
- fit_metric: bfloat16 [512, 512, 512], P(('orb', 'aux'))
- domain: int32 [512, 512], P('orb'), may hold values from 0 to 127, as said below
- counts: int32 [512, 16], P('orb'), may hold values from 16 to 64, as said below
- orbital_ids: int32 [512], P(('orb', 'aux')), may hold values from 0 to 511, each once
- occ_energy: float32 [512], replicated, may hold values from -1.5 to -0.3
- osv_energy: bfloat16 [512, 128], P(('orb', 'aux')), may hold values from 0.29882812 to 3
- matchings: int32 [4, 8], replicated, may hold values from 0 to 7, as said below
- screening: int32 [512, 5, 4], P(('orb', 'aux')), may hold values 0 or 1
Outputs:
- density: float32 [512, 2048, 128], P('orb', 'aux')
- pair_energy: float32 [512, 5, 4], P(('orb', 'aux'))
The draws below stay inside these ranges and needn't reach their ends.
Inputs may be any that keep to these rules, and one draw needn't show every extreme that they name: `counts`: every row sums to 512; every entry is at most 64, and every row has an entry equal to 64. `domain`: the positions of a row are taken by owner 0 first, then owner 1 and so on, in the numbers that counts gives; within one owner's run the entries are distinct. `matchings`: row q maps orb index o to o XOR m_q, with a mask m_q from 1 to 7; rounds may repeat a mask.
All inputs are finite; a program needn't handle non-finite values. No bound on the sum of `screening` on one device may be relied on, other than what follows from the above.
Results may differ from the reference program's by a relative error of at most 0.0029.
Values may be sent and summed in bfloat16 or wider, within the bound.
No kernel may reach another device: no remote copies, remote signals or barrier semaphores. Data moves between devices by JAX's collectives and lax.ppermute only.
A program may use at most 128 MiB of HBM per device.

```python
import math
import jax
import jax.numpy as jnp
from jax import lax

NOSV = 128
NFIT = 512
OCC_DEV = 4
AUX_DEV = 128
MATCHES = 4
NOCC = 512
NAUX = 2048
CAP = 64
N_ORB = 8
N_AUX = 16
DEVICES = 128


def domain_tables(key):
    key = jax.random.fold_in(key, 5)
    key_owner, key_second, key_extra, key_rows = jax.random.split(key, 4)
    base = NFIT // (2 * N_AUX)
    extra = CAP - base
    spare = NFIT - N_AUX * base - extra
    owner = jnp.minimum(jax.random.randint(key_owner, (NOCC,), 0, N_AUX), jax.random.randint(key_second, (NOCC,), 0, N_AUX)).astype(jnp.int32)
    slots_total = (N_AUX - 1) * extra
    orders = jax.vmap(lambda single: jax.random.permutation(single, slots_total))(jax.random.split(key_extra, NOCC))
    taken = (orders < spare).astype(jnp.int32).reshape(NOCC, N_AUX - 1, extra).sum(axis=2)
    owners = jnp.arange(N_AUX, dtype=jnp.int32)
    ordinal = jnp.clip(owners[None, :] - (owners[None, :] > owner[:, None]).astype(jnp.int32), 0, N_AUX - 2)
    others = jnp.take_along_axis(taken, ordinal, axis=1)
    counts = (base + jnp.where(owners[None, :] == owner[:, None], extra, others)).astype(jnp.int32)
    row_orders = jax.vmap(lambda single: jax.random.permutation(single, AUX_DEV))(jax.random.split(key_rows, NOCC * N_AUX))
    row_orders = row_orders.reshape(NOCC, N_AUX * AUX_DEV).astype(jnp.int32)
    run_ends = jnp.cumsum(counts, axis=1)
    run_starts = run_ends - counts
    positions = jnp.arange(NFIT, dtype=jnp.int32)
    which = jnp.sum((positions[None, :, None] >= run_ends[:, None, :]).astype(jnp.int32), axis=2)
    offset = positions[None, :] - jnp.take_along_axis(run_starts, which, axis=1)
    domain = jnp.take_along_axis(row_orders, which * AUX_DEV + offset, axis=1)
    return (counts, domain.astype(jnp.int32))


def draw_counts(key, part):
    return domain_tables(key)[0]


def draw_domain(key, part):
    return domain_tables(key)[1]


def draw_matchings(key, part):
    key = jax.random.fold_in(key, 17)
    masks = jax.random.randint(key, (MATCHES,), 1, N_ORB).astype(jnp.int32)
    indices = jnp.arange(N_ORB, dtype=jnp.int32)
    return jnp.bitwise_xor(indices[None, :], masks[:, None]).astype(jnp.int32)


def draw_fit_metric(key, part):
    key = jax.random.fold_in(key, 11)
    key_off, key_diag = jax.random.split(key)
    off = jax.random.normal(key_off, (NOCC, NFIT, NFIT), jnp.float32) * (0.5 / math.sqrt(NFIT))
    diag = jax.random.uniform(key_diag, (NOCC, NFIT), jnp.float32, 0.5, 2.0)
    indices = jnp.arange(NFIT, dtype=jnp.int32)
    on_diag = indices[:, None] == indices[None, :]
    return jnp.where(on_diag[None, :, :], diag[:, :, None], off).astype(jnp.bfloat16)


def with_ends(entries, stream_key, smallest, high):
    longest = entries.shape.index(max(entries.shape))
    spots = []
    for shift in (0, 1):
        where = [jax.random.randint(jax.random.fold_in(stream_key, axis), (), 0, length) for axis, length in enumerate(entries.shape)]
        where[longest] = (where[longest] + shift) % entries.shape[longest]
        spots.append(tuple(where))
    return entries.at[spots[0]].set(smallest).at[spots[1]].set(high)


def level_of(rng, dims, cuts, smallest, largest):
    def one(axis_at, blocks):
        steps = jax.random.uniform(jax.random.fold_in(jax.random.fold_in(rng, 6), axis_at), (blocks,), jnp.float32, smallest / len(cuts), largest / len(cuts))
        return jnp.repeat(jnp.exp(steps), dims[axis_at] // blocks).reshape((-1,) + (1,) * (len(dims) - axis_at - 1))

    factor_of = one(*cuts[0])
    for cut in cuts[1:]:
        factor_of = factor_of * one(*cut)
    return factor_of


def noise(stream_key, shape, width, most, cuts=(), kind=jnp.bfloat16):
    drawn = jax.random.normal(stream_key, shape, jnp.float32) * width
    if len(cuts) > 0:
        drawn = level_of(stream_key, shape, cuts, -0.22, 0.18) * drawn
    return jnp.clip(drawn, min=-most, max=most).astype(kind)


def setup_inputs(seed: int = 0) -> dict:
    arg_keys = jax.random.split(jax.random.key(seed), 10)
    raw_rows = noise(arg_keys[0], (NOCC, NAUX, NOSV), (NAUX ** 0.25 / NFIT ** 0.5), 4.0, ((0, 8), (1, 16)))
    fit_metric = draw_fit_metric(jax.random.fold_in(arg_keys[9], 71), 0)
    domain = draw_domain(jax.random.fold_in(arg_keys[9], 71), 0)
    counts = draw_counts(jax.random.fold_in(arg_keys[9], 71), 0)
    orbital_ids = jax.random.permutation(arg_keys[4], NOCC).astype(jnp.int32)
    occ_energy = jnp.clip(jax.random.uniform(arg_keys[5], (NOCC,), jnp.float32, -1.5, -0.3), -1.5, -0.3)
    osv_energy = jnp.clip(jnp.exp(math.log(3.0) - 2.306499 * jax.random.uniform(arg_keys[6], (NOCC, NOSV), jnp.float32) ** level_of(arg_keys[6], (NOCC, NOSV), ((0, 128),), -0.2, 0.2)), 0.29882812, 3.0).astype(jnp.bfloat16)
    matchings = draw_matchings(jax.random.fold_in(arg_keys[9], 71), 0)
    screening = with_ends((jax.random.randint(arg_keys[8], (NOCC, MATCHES + 1, OCC_DEV), 0, 4) < 3).astype(jnp.int32), jax.random.fold_in(arg_keys[8], 1), 0, 1)
    return dict(raw_rows=raw_rows, fit_metric=fit_metric, domain=domain, counts=counts, orbital_ids=orbital_ids, occ_energy=occ_energy, osv_energy=osv_energy, matchings=matchings, screening=screening)


PAIR_SCALE = 1.3


def fit_one(operands):
    return jnp.dot(operands[0], operands[1], preferred_element_type=jnp.float32).astype(jnp.bfloat16)


def reference(raw_rows, fit_metric, domain, counts, orbital_ids, occ_energy, osv_energy, matchings, screening):
    run_ends = jnp.cumsum(counts, axis=1)
    positions = jnp.arange(NFIT, dtype=jnp.int32)
    source = jnp.sum((positions[None, :, None] >= run_ends[:, None, :]).astype(jnp.int32), axis=2)
    rows_global = (source * AUX_DEV + domain).astype(jnp.int32)
    slots_all = jnp.arange(NOCC, dtype=jnp.int32)
    gathered_rows = raw_rows[slots_all[:, None], rows_global]
    fitted = lax.map(fit_one, (fit_metric, gathered_rows))
    occ_values = occ_energy[orbital_ids]
    osv_values = osv_energy.astype(jnp.float32)
    local_range = jnp.arange(OCC_DEV, dtype=jnp.int32)

    def device_work(device):
        orb_index = device // N_AUX
        aux_index = device % N_AUX
        own_slots = device * OCC_DEV + local_range
        raw_full = jnp.zeros((OCC_DEV, NAUX, NOSV), jnp.bfloat16)
        raw_full = raw_full.at[local_range[:, None], rows_global[own_slots]].set(gathered_rows[own_slots])
        partner_devices = jnp.concatenate([device[None], (matchings[:, orb_index] * N_AUX + aux_index).astype(jnp.int32)])
        density = jnp.zeros((OCC_DEV, NAUX, NOSV), jnp.float32)
        energies = []
        for round_index in range(MATCHES + 1):
            partner_slots = partner_devices[round_index] * OCC_DEV + local_range
            far_fitted = fitted[partner_slots].astype(jnp.float32)
            far_rows = rows_global[partner_slots].reshape(-1)
            picked = raw_full[:, far_rows].reshape(OCC_DEV, OCC_DEV, NFIT, NOSV).astype(jnp.float32)
            integrals = jnp.einsum("klpa,lpb->klab", picked, far_fitted)
            denominator = (osv_values[own_slots][:, None, :, None] + osv_values[partner_slots][None, :, None, :]
                           - occ_values[own_slots][:, None, None, None] - occ_values[partner_slots][None, :, None, None])
            screen_round = screening[own_slots, round_index].astype(jnp.float32)
            amplitudes = (screen_round[:, :, None, None] * integrals / denominator).astype(jnp.bfloat16)
            amplitudes = lax.optimization_barrier(amplitudes).astype(jnp.float32)
            energies.append(PAIR_SCALE * jnp.sum(amplitudes * integrals, axis=(2, 3)) / (NOSV * NOSV))
            pieces = jnp.einsum("klab,lpb->klpa", amplitudes, far_fitted)
            density = density.at[:, far_rows].add(pieces.reshape(OCC_DEV, OCC_DEV * NFIT, NOSV))
        return density, jnp.stack(energies, axis=1)

    density, energies = lax.map(device_work, jnp.arange(DEVICES, dtype=jnp.int32))
    return density.reshape(NOCC, NAUX, NOSV), energies.reshape(NOCC, MATCHES + 1, OCC_DEV)
```

```python
import functools

import jax
import jax.numpy as jnp
from jax import lax
from jax.experimental import pallas as pl
from jax.experimental.pallas import tpu as pltpu
from jax.sharding import PartitionSpec as P

PAIR_SCALE = 1.3
BF16 = jnp.bfloat16
F32 = jnp.float32
I32 = jnp.int32
NOSV = 128
NFIT = 512
OCC = 4
AUXD = 128
NAUX_DEV = 16
NAUX = AUXD * NAUX_DEV
CAP = 64
CHUNKS = NFIT // CAP
ENDS = NAUX_DEV + 1
SLAB = OCC * NOSV
VMEM_LIMIT = 50 * 1024 * 1024


def params(**kw):
    return pltpu.CompilerParams(vmem_limit_bytes=VMEM_LIMIT, **kw)


def pack_kernel(table, raw, out):
    lanes = lax.broadcasted_iota(I32, (2 * CAP, 2 * AUXD), 1)
    for pair in range(8):
        column = table[0, :, pair : pair + 1]
        pick = jnp.where(lanes == column, 1.0, 0.0).astype(BF16)
        rows = raw[2 * pair : 2 * pair + 2].reshape(2 * AUXD, NOSV)
        got = jnp.dot(pick, rows, preferred_element_type=F32).astype(BF16)
        out[2 * pair] = got[:CAP]
        out[2 * pair + 1] = got[CAP:]


def pack_rows(raw_rows, domain, run_starts, run_ends, my_aux):
    group = raw_rows.shape[0]
    start = lax.dynamic_slice_in_dim(run_starts, my_aux, 1, 1)[:, :, None]
    end = lax.dynamic_slice_in_dim(run_ends, my_aux, 1, 1)[:, :, None]
    position = jnp.arange(NFIT, dtype=I32).reshape(1, CHUNKS, CAP)
    inside = (position >= start) & (position < end)
    odd = (jnp.arange(group, dtype=I32) % 2 * AUXD)[:, None, None]
    code = domain.reshape(group, CHUNKS, CAP) + odd + 1
    table = jnp.sum(jnp.where(inside, code, 0), axis=1) - 1
    steps = group // 16
    table = table.reshape(steps, 8, 2 * CAP).transpose(0, 2, 1)
    return pl.pallas_call(
        pack_kernel,
        grid=(steps,),
        in_specs=[
            pl.BlockSpec((1, 2 * CAP, 8), lambda i: (i, 0, 0)),
            pl.BlockSpec((16, AUXD, NOSV), lambda i: (i, 0, 0)),
        ],
        out_specs=pl.BlockSpec((16, CAP, NOSV), lambda i: (i, 0, 0)),
        out_shape=jax.ShapeDtypeStruct((group, CAP, NOSV), BF16),
        compiler_params=params(),
        name="pack_rows",
    )(table, raw_rows)


def fit_kernel(ends, received, metric, fitted, block, acc):
    k = pl.program_id(0)
    acc[...] = jnp.zeros(acc.shape, F32)
    sub = lax.broadcasted_iota(I32, (CAP, NOSV), 0)
    for a in range(NAUX_DEV):
        start = ends[k * ENDS + a]
        at = pl.multiple_of(jnp.minimum(start // CAP, CHUNKS - 1) * CAP, CAP)
        first = start % CAP
        rows = received[a, 0].astype(F32)
        acc[pl.ds(at, CAP), :] += jnp.where(sub >= first, rows, 0.0)
        acc[pl.ds(at + CAP, CAP), :] += jnp.where(sub >= first, 0.0, rows)
    whole = acc[:NFIT, :].astype(BF16)
    block[0] = whole
    fitted[0] = jnp.dot(metric[0], whole, preferred_element_type=F32).astype(BF16)


def fit(ends, received, metric):
    shape = jax.ShapeDtypeStruct((OCC, NFIT, NOSV), BF16)
    return pl.pallas_call(
        fit_kernel,
        grid_spec=pltpu.PrefetchScalarGridSpec(
            num_scalar_prefetch=1,
            grid=(OCC,),
            in_specs=[
                pl.BlockSpec((NAUX_DEV, 1, CAP, NOSV), lambda k, e: (0, k, 0, 0)),
                pl.BlockSpec((1, NFIT, NFIT), lambda k, e: (k, 0, 0)),
            ],
            out_specs=[
                pl.BlockSpec((1, NFIT, NOSV), lambda k, e: (k, 0, 0)),
                pl.BlockSpec((1, NFIT, NOSV), lambda k, e: (k, 0, 0)),
            ],
            scratch_shapes=[pltpu.VMEM((NFIT + CAP, NOSV), F32)],
        ),
        out_shape=[shape, shape],
        compiler_params=params(),
        name="fit",
    )(ends, received, metric)


def spread_rows(source, slot, table_at, windows, ends, store):
    sub = lax.broadcasted_iota(I32, (AUXD, 2 * CAP), 0)
    lane = lax.broadcasted_iota(I32, (1, 2 * CAP), 1)
    for a in range(NAUX_DEV):
        start = ends[table_at * ENDS + a]
        end = ends[table_at * ENDS + a + 1]
        chunk = jnp.minimum(start // CAP, CHUNKS - 2)
        at = pl.multiple_of(chunk * CAP, CAP)
        row = windows[table_at, pl.ds(chunk, 1), :]
        row = jnp.where((lane >= start - at) & (lane < end - at), row, -1)
        pick = jnp.where(sub == row, 1.0, 0.0).astype(BF16)
        rows = source[slot, pl.ds(at, 2 * CAP), :]
        store(a, jnp.dot(pick, rows, preferred_element_type=F32))


def one_round(
    q, table0, source, ends, screen, windows, far_energy, own_energy, raw_t, spread, ints, amps, den, energy, first
):
    for l in range(OCC):

        def store(a, value, l=l):
            spread[a * AUXD : (a + 1) * AUXD, l * NOSV : (l + 1) * NOSV] = value.astype(BF16)

        spread_rows(source, l, table0 + l, windows, ends, store)
    ints[...] = jnp.dot(raw_t[...], spread[...], preferred_element_type=F32)
    for k in range(OCC):
        for l in range(OCC):
            ks = slice(k * NOSV, (k + 1) * NOSV)
            ls = slice(l * NOSV, (l + 1) * NOSV)
            value = ints[ks, ls]
            denominator = own_energy[ks, :] + far_energy[pl.ds(table0 + l, 1), :]
            amp = (screen[(k * 5 + q) * OCC + l] * value / denominator).astype(BF16)
            amps[ks, ls] = amp
            part = jnp.sum(amp.astype(F32) * value, axis=0, keepdims=True)
            energy[q, k * OCC + l : k * OCC + l + 1, :] = part
    tile = 512
    for m in range(NAUX // tile):
        ms = slice(m * tile, (m + 1) * tile)
        value = lax.dot_general(
            spread[ms, :], amps[...], (((1,), (1,)), ((), ())), preferred_element_type=F32
        )
        den[ms, :] = value if first else den[ms, :] + value


def own_kernel(
    ends, screen, windows, far_energy, own_energy, block, fitted, raw_out, den_out, energy,
    spread, ints, amps, sems,
):
    for k in range(OCC):

        def store(a, value, k=k):
            raw_out[k * NOSV : (k + 1) * NOSV, a * AUXD : (a + 1) * AUXD] = value.T.astype(BF16)

        spread_rows(block, k, k, windows, ends, store)
    energy[...] = jnp.zeros(energy.shape, F32)
    one_round(
        0, 0, fitted, ends, screen, windows, far_energy, own_energy, raw_out, spread, ints, amps, den_out, energy, True
    )


def own_round(ends, screen, windows, far_energy, own_energy, block, fitted):
    smem = pl.BlockSpec(memory_space=pltpu.SMEM)
    vmem = pl.BlockSpec(memory_space=pltpu.VMEM)
    return pl.pallas_call(
        own_kernel,
        in_specs=[smem, smem] + [vmem] * 5,
        out_specs=[vmem] * 3,
        out_shape=[
            jax.ShapeDtypeStruct((SLAB, NAUX), BF16),
            jax.ShapeDtypeStruct((NAUX, SLAB), F32),
            jax.ShapeDtypeStruct((5, 16, NOSV), F32),
        ],
        scratch_shapes=[
            pltpu.VMEM((NAUX, SLAB), BF16),
            pltpu.VMEM((SLAB, SLAB), F32),
            pltpu.VMEM((SLAB, SLAB), BF16),
            pltpu.SemaphoreType.DMA((2,)),
        ],
        compiler_params=params(),
        name="own_round",
    )(ends, screen, windows, far_energy, own_energy, block, fitted)


def phase_kernel(
    masks, last, pieces, rounds, ends, screen, windows, far_energy, own_energy, raw_in, den_in, *rest
):
    far = rest[: len(pieces)]
    den_out, energy, raw_t, den, source, spread, ints, amps, sems = rest[len(pieces) :]

    def wanted(mask):
        found = mask == masks[0]
        for other in masks[1:]:
            found |= mask == other
        return found

    count = wanted(rounds[0]).astype(I32)
    for q in range(1, 4):
        count += wanted(rounds[q]).astype(I32)
    energy[...] = jnp.zeros(energy.shape, F32)

    load_den = pltpu.make_async_copy(den_in, den, sems.at[0])
    load_raw = pltpu.make_async_copy(raw_in, raw_t, sems.at[1])

    def work():
        load_den.start()
        load_raw.start()
        load_den.wait()
        load_raw.wait()

        def body(q, carry):
            mask = rounds[q]

            @pl.when(wanted(mask))
            def _():
                for mask_at, piece_list in zip(masks, pieces_of(pieces, masks)):

                    @pl.when(mask == mask_at)
                    def _(piece_list=piece_list):
                        for index, lo, hi in piece_list:
                            copy = pltpu.make_async_copy(far[index], source.at[pl.ds(lo, hi - lo)], sems.at[2])
                            copy.start()
                            copy.wait()

                one_round(
                    q + 1, rounds[4 + q] * OCC, source, ends, screen, windows, far_energy, own_energy,
                    raw_t, spread, ints, amps, den, energy, False,
                )

            return carry

        lax.fori_loop(0, 4, body, 0)

    if last:
        work()
        for a in range(NAUX_DEV):
            for k in range(OCC):
                den_out[a, k] = den[a * AUXD : (a + 1) * AUXD, k * NOSV : (k + 1) * NOSV].astype(BF16)
    else:

        @pl.when(count > 0)
        def _():
            work()
            save = pltpu.make_async_copy(den, den_out, sems.at[0])
            save.start()
            save.wait()


def pieces_of(pieces, masks):
    return [[p[1:] for p in pieces_entry(pieces) if p[0] == mask] for mask in masks]


def pieces_entry(pieces):
    return [(mask, index, lo, hi) for index, (mask, lo, hi) in enumerate(pieces)]


def phase(masks, last, pieces, rounds, ends, screen, windows, far_energy, own_energy, raw_t, den, far):
    smem = pl.BlockSpec(memory_space=pltpu.SMEM)
    vmem = pl.BlockSpec(memory_space=pltpu.VMEM)
    hbm = pl.BlockSpec(memory_space=pl.ANY)
    if last:
        den_shape = jax.ShapeDtypeStruct((NAUX_DEV, OCC, AUXD, NOSV), BF16)
        den_spec = vmem
        alias = {}
    else:
        den_shape = jax.ShapeDtypeStruct((NAUX, SLAB), F32)
        den_spec = hbm
        alias = {7: 0}
    return pl.pallas_call(
        functools.partial(phase_kernel, masks, last, pieces),
        in_specs=[smem, smem, smem, vmem, vmem, vmem, hbm, hbm] + [hbm] * len(far),
        out_specs=[den_spec, vmem],
        out_shape=[den_shape, jax.ShapeDtypeStruct((5, 16, NOSV), F32)],
        scratch_shapes=[
            pltpu.VMEM((SLAB, NAUX), BF16),
            pltpu.VMEM((NAUX, SLAB), F32),
            pltpu.VMEM((OCC, NFIT, NOSV), BF16),
            pltpu.VMEM((NAUX, SLAB), BF16),
            pltpu.VMEM((SLAB, SLAB), F32),
            pltpu.VMEM((SLAB, SLAB), BF16),
            pltpu.SemaphoreType.DMA((3,)),
        ],
        input_output_aliases=alias,
        compiler_params=params(),
        name="phase_" + "_".join(str(m) for m in masks),
    )(rounds, ends, screen, windows, far_energy, own_energy, raw_t, den, *far)


def tables(meta):
    n = meta.shape[0]
    slots = meta.reshape(n * OCC, 8, NOSV)
    dom = slots[:, :4].reshape(n * OCC, CHUNKS, CAP).astype(I32)
    after = jnp.concatenate([dom[:, 1:], dom[:, :1]], axis=1)
    windows = jnp.concatenate([dom, after], axis=2)
    counts = slots[:, 4, :NAUX_DEV]
    below = jnp.arange(NAUX_DEV)[None, :] < jnp.arange(ENDS)[:, None]
    ends = jnp.sum(jnp.where(below[None], counts[:, None, :], 0.0), axis=2).astype(I32)
    return windows, ends.reshape(-1), slots[:, 5] - slots[:, 6]


def flip(x, mask):
    return lax.ppermute(x, "orb", [(i, i ^ mask) for i in range(lax.axis_size("orb"))])


def per_device(
    raw_rows, fit_metric, domain, counts, orbital_ids, occ_energy, osv_energy, matchings, screening
):
    my_aux = lax.axis_index("aux")
    my_orb = lax.axis_index("orb")
    group = raw_rows.shape[0]
    own_domain = lax.dynamic_slice_in_dim(domain, my_aux * OCC, OCC, 0)
    own_counts = lax.dynamic_slice_in_dim(counts, my_aux * OCC, OCC, 0)
    everyone = jnp.arange(occ_energy.shape[0], dtype=I32)
    own_occ = jnp.sum(
        jnp.where(orbital_ids[:, None] == everyone[None, :], occ_energy[None, :], 0.0), axis=1
    )
    own_osv = osv_energy.astype(F32)
    meta = jnp.concatenate(
        [
            own_domain.astype(F32).reshape(OCC, 4, NOSV),
            jnp.pad(own_counts.astype(F32), ((0, 0), (0, NOSV - NAUX_DEV)))[:, None, :],
            own_osv[:, None, :],
            jnp.broadcast_to(own_occ[:, None, None], (OCC, 2, NOSV)),
        ],
        axis=1,
    )
    everywhere = lax.all_gather(meta, "orb", axis=0)
    own_windows, own_ends, own_term = tables(meta[None])
    windows, ends, far_energy = tables(everywhere)
    own_energy = jnp.broadcast_to(own_term.reshape(SLAB, 1), (SLAB, NOSV))
    screen = screening.astype(F32).reshape(-1)
    rounds = jnp.concatenate(
        [matchings[:, 0], lax.dynamic_index_in_dim(matchings, my_orb, 1, keepdims=False)]
    )

    upto = jnp.arange(NAUX_DEV)[None, :] <= jnp.arange(NAUX_DEV)[:, None]
    run_ends = jnp.sum(jnp.where(upto[None], counts[:, None, :], 0), axis=2)
    packed = pack_rows(raw_rows, domain, run_ends - counts, run_ends, my_aux)
    packed = packed.reshape(NAUX_DEV, OCC, CAP, NOSV)
    received = lax.all_to_all(packed, "aux", split_axis=0, concat_axis=0, tiled=True)
    fitted, block = fit(own_ends, received, fit_metric)

    far1, far2, far6 = flip(fitted, 1), flip(fitted, 2), flip(fitted, 6)
    raw_t, den, energy0 = own_round(
        own_ends, screen, own_windows, own_term, own_energy, block, fitted
    )
    far3, far4, far7 = flip(far2, 1), flip(far6, 2), flip(far1, 6)
    common = (rounds, ends, screen, windows, far_energy, own_energy, raw_t)
    den, energy1 = phase(
        (1, 2, 6), False, ((1, 0, 4), (2, 0, 4), (6, 0, 4)), *common, den, (far1, far2, far6)
    )
    far5 = (flip(far4[0:1], 1), flip(far7[1:2], 2), flip(far3[2:4], 6))
    den, energy2 = phase(
        (3, 4, 7), False, ((3, 0, 4), (4, 0, 4), (7, 0, 4)), *common, den, (far3, far4, far7)
    )
    sent, energy3 = phase((5,), True, ((5, 0, 1), (5, 1, 2), (5, 2, 4)), *common, den, far5)
    returned = lax.all_to_all(sent, "aux", split_axis=0, concat_axis=0, tiled=True)
    density = returned.reshape(group, AUXD, NOSV).astype(F32)
    total = jnp.sum(energy0 + energy1 + energy2 + energy3, axis=2)
    energies = total.reshape(5, OCC, OCC).transpose(1, 0, 2) * (PAIR_SCALE / (NOSV * NOSV))
    return density, energies


def solution(mesh):
    placed = (
        P("orb", "aux", None),
        P(("orb", "aux"), None, None),
        P("orb", None),
        P("orb", None),
        P(("orb", "aux")),
        P(),
        P(("orb", "aux"), None),
        P(),
        P(("orb", "aux"), None, None),
    )
    return jax.shard_map(
        per_device,
        mesh=mesh,
        in_specs=placed,
        out_specs=(P("orb", "aux", None), P(("orb", "aux"), None, None)),
        check_vma=False,
    )
```

```python
import functools

import jax
import jax.numpy as jnp
from jax import lax
from jax.experimental import pallas as pl
from jax.experimental.pallas import tpu as pltpu
from jax.sharding import PartitionSpec as P

PAIR_SCALE = 1.3
BF16 = jnp.bfloat16
F32 = jnp.float32
I32 = jnp.int32
NOSV = 128
NFIT = 512
OCC = 4
AUXD = 128
NAUX_DEV = 16
NAUX = AUXD * NAUX_DEV
CAP = 64
CHUNKS = NFIT // CAP
TAIL = 32
ROWS = NFIT + TAIL
TILE = 512
SLAB = OCC * NOSV
VMEM_LIMIT = 50 * 1024 * 1024


def params(**kw):
    return pltpu.CompilerParams(vmem_limit_bytes=VMEM_LIMIT, **kw)


def pack_kernel(where_am_i, domain, counts, raw, out, columns):
    step = pl.program_id(0)

    @pl.when(step == 0)
    def _():
        me = where_am_i[0]
        owner = lax.broadcasted_iota(I32, (64, NAUX_DEV), 1)
        start = jnp.sum(jnp.where(owner < me, counts[...], 0), axis=1, keepdims=True)
        end = start + jnp.sum(jnp.where(owner == me, counts[...], 0), axis=1, keepdims=True)
        lane = lax.broadcasted_iota(I32, (64, NOSV), 1)
        code = jnp.zeros((64, NOSV), I32)
        for part in range(4):
            position = lane + part * NOSV
            inside = (position >= start) & (position < end)
            code += jnp.where(inside, domain[:, part * NOSV : (part + 1) * NOSV] + 1, 0)
        code = (code + pltpu.roll(code, CAP, 1) - 1).astype(F32)
        turned = jnp.concatenate([code, code], axis=0).T
        odd = lax.broadcasted_iota(I32, (NOSV, NOSV), 1) % 2 == 1
        turned = jnp.where(odd & (turned >= 0.0), turned + AUXD, turned)
        for part in range(4):
            columns[part] = turned[:, 16 * part : 16 * part + 16]

    lanes = lax.broadcasted_iota(I32, (2 * CAP, 2 * AUXD), 1).astype(F32)
    upper = lax.broadcasted_iota(I32, (2 * CAP, 1), 0) < CAP
    mine = columns[step]
    for pair in range(8):
        column = jnp.where(upper, mine[:, 2 * pair : 2 * pair + 1], mine[:, 2 * pair + 1 : 2 * pair + 2])
        pick = jnp.where(lanes == column, 1.0, 0.0).astype(BF16)
        rows = raw[2 * pair : 2 * pair + 2].reshape(2 * AUXD, NOSV)
        got = jnp.dot(pick, rows, preferred_element_type=F32).astype(BF16)
        out[2 * pair] = got[:CAP]
        out[2 * pair + 1] = got[CAP:]


def pack_rows(where_am_i, domain, counts, raw_rows):
    group = raw_rows.shape[0]
    return pl.pallas_call(
        pack_kernel,
        grid_spec=pltpu.PrefetchScalarGridSpec(
            num_scalar_prefetch=1,
            grid=(group // 16,),
            in_specs=[
                pl.BlockSpec(domain.shape, lambda i, s: (0, 0)),
                pl.BlockSpec(counts.shape, lambda i, s: (0, 0)),
                pl.BlockSpec((16, AUXD, NOSV), lambda i, s: (i, 0, 0)),
            ],
            out_specs=pl.BlockSpec((16, CAP, NOSV), lambda i, s: (i, 0, 0)),
            scratch_shapes=[pltpu.VMEM((4, NOSV, 16), F32)],
        ),
        out_shape=jax.ShapeDtypeStruct((group, CAP, NOSV), BF16),
        compiler_params=params(),
        name="pack_rows",
    )(where_am_i, domain, counts, raw_rows)


def tables_kernel(where_am_i, counts, ids, occ, domain, osv, out, windows, table):
    me = where_am_i[0]
    lane = lax.broadcasted_iota(I32, (1, NOSV), 1)
    energies = osv[...].astype(F32)
    for k in range(OCC):
        row = domain[pl.ds(me * OCC + k, 1), :]
        for i in range(4):
            windows[2 * i : 2 * i + 1, :] = row[:, i * NOSV : (i + 1) * NOSV]
            if i < 3:
                windows[2 * i + 1 : 2 * i + 2, :] = row[:, i * NOSV + CAP : (i + 1) * NOSV + CAP]
        table[...] = jnp.zeros(table.shape, F32)
        starts = jnp.zeros((1, NOSV), I32)
        start = jnp.int32(0)
        for a in range(NAUX_DEV):
            end = start + counts[me * OCC + k, a]
            chunk = jnp.minimum(start // CAP, CHUNKS - 2)
            at = chunk * CAP
            entry = windows[pl.ds(chunk, 1), :]
            entry = jnp.where((lane >= start - at) & (lane < end - at), entry, -1)
            table[a : a + 1, :] = entry.astype(F32)
            starts = jnp.where(lane == a, at, starts)
            start = end
        table[16:17, :] = starts.astype(F32)
        term = energies[k : k + 1, :] - occ[ids[k]]
        for i in range(3):
            rounded = term.astype(BF16).astype(F32)
            table[17 + i : 18 + i, :] = rounded
            term = term - rounded
        out[k] = table[...].astype(BF16)


def slot_tables(where_am_i, counts, ids, occ, domain, osv):
    smem = pl.BlockSpec(memory_space=pltpu.SMEM)
    vmem = pl.BlockSpec(memory_space=pltpu.VMEM)
    return pl.pallas_call(
        tables_kernel,
        in_specs=[smem, smem, smem, smem, vmem, vmem],
        out_specs=vmem,
        out_shape=jax.ShapeDtypeStruct((OCC, TAIL, NOSV), BF16),
        scratch_shapes=[pltpu.VMEM((8, NOSV), I32), pltpu.VMEM((TAIL, NOSV), F32)],
        compiler_params=params(),
        name="slot_tables",
    )(where_am_i, counts, ids, occ, domain, osv)


def fit_kernel(where_am_i, counts, received, metric, tail, fitted, block, acc):
    k = pl.program_id(0)
    acc[...] = jnp.zeros(acc.shape, F32)
    sub = lax.broadcasted_iota(I32, (CAP, NOSV), 0)
    start = jnp.int32(0)
    for a in range(NAUX_DEV):
        at = pl.multiple_of(jnp.minimum(start // CAP, CHUNKS - 1) * CAP, CAP)
        first = start % CAP
        rows = received[a, 0].astype(F32)
        acc[pl.ds(at, CAP), :] += jnp.where(sub >= first, rows, 0.0)
        acc[pl.ds(at + CAP, CAP), :] += jnp.where(sub >= first, 0.0, rows)
        start += counts[where_am_i[0] * OCC + k, a]
    whole = acc[:NFIT, :].astype(BF16)
    block[0] = whole
    fitted[0, :NFIT] = jnp.dot(metric[0], whole, preferred_element_type=F32).astype(BF16)
    fitted[0, NFIT:] = tail[0]


def fit(where_am_i, counts, received, metric, tail):
    def one(shape):
        return pl.BlockSpec((1,) + shape, lambda k, s: (k, 0, 0))

    return pl.pallas_call(
        fit_kernel,
        grid_spec=pltpu.PrefetchScalarGridSpec(
            num_scalar_prefetch=1,
            grid=(OCC,),
            in_specs=[
                pl.BlockSpec(memory_space=pltpu.SMEM),
                pl.BlockSpec((NAUX_DEV, 1, CAP, NOSV), lambda k, s: (0, k, 0, 0)),
                one((NFIT, NFIT)),
                one((TAIL, NOSV)),
            ],
            out_specs=[one((ROWS, NOSV)), one((NFIT, NOSV))],
            scratch_shapes=[pltpu.VMEM((NFIT + CAP, NOSV), F32)],
        ),
        out_shape=[
            jax.ShapeDtypeStruct((OCC, ROWS, NOSV), BF16),
            jax.ShapeDtypeStruct((OCC, NFIT, NOSV), BF16),
        ],
        compiler_params=params(),
        name="fit",
    )(where_am_i, counts, received, metric, tail)


def spread_rows(source, table, starts, at_slot, store):
    sub = lax.broadcasted_iota(I32, (AUXD, 2 * CAP), 0).astype(F32)
    for a in range(NAUX_DEV):
        at = pl.multiple_of(starts[at_slot, a], CAP)
        pick = jnp.where(sub == table[a : a + 1, :], 1.0, 0.0).astype(BF16)
        store(a, jnp.dot(pick, source[pl.ds(at, 2 * CAP), :], preferred_element_type=F32))


def energy_of(tail):
    return tail[1:2, :] + tail[2:3, :] + tail[3:4, :]


def read_starts(sources, starts_v, starts_s, sem):
    for i, source in enumerate(sources):
        starts_v[i : i + 1, :] = source[NFIT + 16 :, :].astype(F32)[0:1, :].astype(I32)
    copy = pltpu.make_async_copy(starts_v, starts_s, sem)
    copy.start()
    copy.wait()


def own_columns(tails):
    rows = [energy_of(t) for t in tails]
    return jnp.concatenate(rows + rows, axis=0).T


def one_round(
    q, slot_of, starts, at_slot, screening, columns, raw_t, spread, ints, amps, energy, accumulate
):
    terms = []
    for l in range(OCC):

        def store(a, value, l=l):
            spread[a * AUXD : (a + 1) * AUXD, l * NOSV : (l + 1) * NOSV] = value.astype(BF16)

        source = slot_of(l)
        tail = source[NFIT:, :].astype(F32)
        terms.append(energy_of(tail[16:, :]))
        spread_rows(source, tail, starts, at_slot + l, store)
    ints[...] = jnp.dot(raw_t[...], spread[...], preferred_element_type=F32)
    for k in range(OCC):
        for l in range(OCC):
            ks = slice(k * NOSV, (k + 1) * NOSV)
            ls = slice(l * NOSV, (l + 1) * NOSV)
            value = ints[ks, ls]
            denominator = columns[:, k : k + 1] + terms[l]
            amp = (screening[k, q, l].astype(F32) * value / denominator).astype(BF16)
            amps[ks, ls] = amp
            part = jnp.sum(amp.astype(F32) * value, axis=0, keepdims=True)
            energy[q, k * OCC + l : k * OCC + l + 1, :] = part
    for m in range(NAUX // TILE):
        rows = spread[m * TILE : (m + 1) * TILE, :]
        accumulate(
            m,
            lax.dot_general(
                rows, amps[...], (((1,), (1,)), ((), ())), preferred_element_type=F32
            ),
        )


def tile_copy(m, source, target, sems):
    rows = pl.ds(m * TILE, TILE)
    return pltpu.make_async_copy(source.at[rows], target.at[rows], sems.at[m])


def own_kernel(
    screening, fitted, block, raw_out, den_out, energy,
    den, starts_v, starts_s, spread, ints, amps, sems, sem,
):
    read_starts([fitted.at[k] for k in range(OCC)], starts_v, starts_s, sem.at[0])
    for k in range(OCC):

        def store(a, value, k=k):
            raw_out[k * NOSV : (k + 1) * NOSV, a * AUXD : (a + 1) * AUXD] = value.T.astype(BF16)

        spread_rows(block.at[k], fitted[k, NFIT:, :].astype(F32), starts_s, k, store)
    energy[...] = jnp.zeros(energy.shape, F32)
    columns = own_columns([fitted[k, NFIT + 16 :, :].astype(F32) for k in range(OCC)])

    def accumulate(m, value):
        den[m * TILE : (m + 1) * TILE, :] = value
        tile_copy(m, den, den_out, sems).start()

    one_round(
        0, lambda l: fitted.at[l], starts_s, 0, screening, columns, raw_out, spread, ints, amps, energy, accumulate
    )
    for m in range(NAUX // TILE):
        tile_copy(m, den, den_out, sems).wait()


def round_scratch():
    return [
        pltpu.VMEM((NAUX, SLAB), BF16),
        pltpu.VMEM((SLAB, SLAB), F32),
        pltpu.VMEM((SLAB, SLAB), BF16),
        pltpu.SemaphoreType.DMA((NAUX // TILE,)),
    ]


def own_round(screening, fitted, block):
    smem = pl.BlockSpec(memory_space=pltpu.SMEM)
    vmem = pl.BlockSpec(memory_space=pltpu.VMEM)
    hbm = pl.BlockSpec(memory_space=pl.ANY)
    return pl.pallas_call(
        own_kernel,
        in_specs=[smem, vmem, vmem],
        out_specs=[vmem, hbm, vmem],
        out_shape=[
            jax.ShapeDtypeStruct((SLAB, NAUX), BF16),
            jax.ShapeDtypeStruct((NAUX, SLAB), F32),
            jax.ShapeDtypeStruct((5, 16, NOSV), F32),
        ],
        scratch_shapes=[
            pltpu.VMEM((NAUX, SLAB), F32),
            pltpu.VMEM((8, NOSV), I32),
            pltpu.SMEM((8, NOSV), I32),
        ]
        + round_scratch()
        + [pltpu.SemaphoreType.DMA((1,))],
        compiler_params=params(),
        name="own_round",
    )(screening, fitted, block)


def phase_kernel(masks, last, pieces, matchings, screening, own_tail, raw_t, den_in, *rest):
    far = rest[: len(pieces)]
    rest = rest[len(pieces) :]
    den_out, energy, den, source, starts_v, starts_s = rest[:6]
    rest = rest[6:]
    if last:
        short = rest[0]
        rest = rest[1:]
    spread, ints, amps, sems, piece_sems, sem = rest
    tiles = NAUX // TILE

    def wanted(mask):
        found = mask == masks[0]
        for other in masks[1:]:
            found |= mask == other
        return found

    wants = [wanted(matchings[q, 0]).astype(I32) for q in range(4)]
    count = wants[0] + wants[1] + wants[2] + wants[3]
    energy[...] = jnp.zeros(energy.shape, F32)
    loads = [tile_copy(m, den_in, den, sems) for m in range(tiles)]

    def fetch(index):
        mask, lo, hi = pieces[index]
        target = source.at[masks.index(mask), pl.ds(lo, hi - lo)]
        return pltpu.make_async_copy(far[index], target, piece_sems.at[index])

    def rounds():
        for index in range(len(pieces)):
            fetch(index).start()
        for index in range(len(pieces)):
            fetch(index).wait()
        slots = [source.at[i, l] for i in range(len(masks)) for l in range(OCC)]
        read_starts(slots, starts_v, starts_s, sem.at[0])
        columns = own_columns([own_tail[k, 16:, :].astype(F32) for k in range(OCC)])

        def body(q, done):
            mask = matchings[q, 0]

            @pl.when(wanted(mask))
            def _():
                which = jnp.int32(0)
                for i in range(1, len(masks)):
                    which = jnp.where(mask == masks[i], i, which)

                def accumulate(m, value):
                    @pl.when(done == 0)
                    def _():
                        loads[m].wait()

                    rows = pl.ds(m * TILE, TILE)
                    den[rows, :] = den[rows, :] + value
                    if not last:

                        @pl.when(done == count - 1)
                        def _():
                            tile_copy(m, den, den_out, sems).start()

                one_round(
                    q + 1, lambda l: source.at[which, l], starts_s, which * OCC, screening, columns,
                    raw_t, spread, ints, amps, energy, accumulate,
                )

            return done + wanted(mask).astype(I32)

        lax.fori_loop(0, 4, body, jnp.int32(0))

    if last:
        for load in loads:
            load.start()

        @pl.when(count > 0)
        def _():
            rounds()

        @pl.when(count == 0)
        def _():
            for load in loads:
                load.wait()

        each = NAUX_DEV // tiles
        sends = []
        for m in range(tiles):
            for a in range(m * each, (m + 1) * each):
                for k in range(OCC):
                    short[a, k] = den[a * AUXD : (a + 1) * AUXD, k * NOSV : (k + 1) * NOSV].astype(BF16)
            owners = pl.ds(m * each, each)
            send = pltpu.make_async_copy(short.at[owners], den_out.at[owners], sems.at[m])
            send.start()
            sends.append(send)
        for send in sends:
            send.wait()
    else:

        @pl.when(count > 0)
        def _():
            for load in loads:
                load.start()
            rounds()
            for m in range(tiles):
                tile_copy(m, den, den_out, sems).wait()


def phase(masks, last, pieces, matchings, screening, own_tail, raw_t, den, far):
    smem = pl.BlockSpec(memory_space=pltpu.SMEM)
    vmem = pl.BlockSpec(memory_space=pltpu.VMEM)
    hbm = pl.BlockSpec(memory_space=pl.ANY)
    if last:
        den_shape = jax.ShapeDtypeStruct((NAUX_DEV, OCC, AUXD, NOSV), BF16)
        more = [pltpu.VMEM((NAUX_DEV, OCC, AUXD, NOSV), BF16)]
        alias = {}
    else:
        den_shape = jax.ShapeDtypeStruct((NAUX, SLAB), F32)
        more = []
        alias = {4: 0}
    rows = -(-len(masks) * OCC // 8) * 8
    return pl.pallas_call(
        functools.partial(phase_kernel, masks, last, pieces),
        in_specs=[smem, smem, vmem, vmem, hbm] + [hbm] * len(far),
        out_specs=[hbm, vmem],
        out_shape=[den_shape, jax.ShapeDtypeStruct((5, 16, NOSV), F32)],
        scratch_shapes=[
            pltpu.VMEM((NAUX, SLAB), F32),
            pltpu.VMEM((len(masks), OCC, ROWS, NOSV), BF16),
            pltpu.VMEM((rows, NOSV), I32),
            pltpu.SMEM((rows, NOSV), I32),
        ]
        + more
        + round_scratch()
        + [pltpu.SemaphoreType.DMA((len(pieces),)), pltpu.SemaphoreType.DMA((1,))],
        input_output_aliases=alias,
        compiler_params=params(),
        name="phase_" + "_".join(str(m) for m in masks),
    )(matchings, screening, own_tail, raw_t, den, *far)


def flip(x, mask):
    return lax.ppermute(x, "orb", [(i, i ^ mask) for i in range(lax.axis_size("orb"))])


def per_device(
    raw_rows, fit_metric, domain, counts, orbital_ids, occ_energy, osv_energy, matchings, screening
):
    where_am_i = lax.axis_index("aux").astype(I32).reshape(1)
    group = raw_rows.shape[0]
    packed = pack_rows(where_am_i, domain, counts, raw_rows)
    packed = packed.reshape(NAUX_DEV, OCC, CAP, NOSV)
    received = lax.all_to_all(packed, "aux", split_axis=0, concat_axis=0, tiled=True)
    tail = slot_tables(where_am_i, counts, orbital_ids, occ_energy, domain, osv_energy)
    fitted, block = fit(where_am_i, counts, received, fit_metric, tail)

    near = (flip(fitted, 1), flip(fitted, 2), flip(fitted, 6))
    raw_t, den, energy0 = own_round(screening, fitted, block)
    near, den = lax.optimization_barrier((near, den))
    far1, far2, far6 = near
    middle = (flip(far2, 1), flip(far6, 2), flip(far1, 6))
    common = (matchings, screening, tail, raw_t)
    den, energy1 = phase((1, 2, 6), False, ((1, 0, 4), (2, 0, 4), (6, 0, 4)), *common, den, near)
    middle, den = lax.optimization_barrier((middle, den))
    far3, far4, far7 = middle
    far5 = (flip(far4[0:1], 1), flip(far7[1:2], 2), flip(far3[2:4], 6))
    den, energy2 = phase((3, 4, 7), False, ((3, 0, 4), (4, 0, 4), (7, 0, 4)), *common, den, middle)
    sent, energy3 = phase((5,), True, ((5, 0, 1), (5, 1, 2), (5, 2, 4)), *common, den, far5)
    returned = lax.all_to_all(sent, "aux", split_axis=0, concat_axis=0, tiled=True)
    density = returned.reshape(group, AUXD, NOSV).astype(F32)
    total = jnp.sum(energy0 + energy1 + energy2 + energy3, axis=2)
    energies = total.reshape(5, OCC, OCC).transpose(1, 0, 2) * (PAIR_SCALE / (NOSV * NOSV))
    return density, energies


def solution(mesh):
    placed = (
        P("orb", "aux", None),
        P(("orb", "aux"), None, None),
        P("orb", None),
        P("orb", None),
        P(("orb", "aux")),
        P(),
        P(("orb", "aux"), None),
        P(),
        P(("orb", "aux"), None, None),
    )
    return jax.shard_map(
        per_device,
        mesh=mesh,
        in_specs=placed,
        out_specs=(P("orb", "aux", None), P(("orb", "aux"), None, None)),
        check_vma=False,
    )
```

```python
import functools

import jax
import jax.numpy as jnp
from jax import lax
from jax.experimental import pallas as pl
from jax.experimental.pallas import tpu as pltpu
from jax.sharding import PartitionSpec as P

PAIR_SCALE = 1.3
BF16 = jnp.bfloat16
F32 = jnp.float32
I32 = jnp.int32
NOSV = 128
NFIT = 512
OCC = 4
AUXD = 128
NAUX_DEV = 16
NAUX = AUXD * NAUX_DEV
CAP = 64
CHUNKS = NFIT // CAP
TAIL = 32
ROWS = NFIT + TAIL
TILE = 512
PARTS = 4
SLAB = OCC * NOSV
VMEM_LIMIT = 28 * 1024 * 1024


def params(**kw):
    return pltpu.CompilerParams(vmem_limit_bytes=VMEM_LIMIT, **kw)


def pack_kernel(where_am_i, domain, counts, raw, out, rows, packed, columns, in_sems, out_sems):
    group = raw.shape[0]
    part = group // PARTS

    def load(i):
        span = pl.ds(i * part, part)
        return pltpu.make_async_copy(raw.at[span], rows.at[span], in_sems.at[i])

    def save(i):
        span = pl.ds(i * part, part)
        return pltpu.make_async_copy(packed.at[span], out.at[span], out_sems.at[i])

    for i in range(PARTS):
        load(i).start()
    me = where_am_i[0]
    owner = lax.broadcasted_iota(I32, (NAUX_DEV, group), 0)
    start = jnp.sum(jnp.where(owner < me, counts[...], 0), axis=0, keepdims=True)
    size = jnp.sum(jnp.where(owner == me, counts[...], 0), axis=0, keepdims=True)
    both = jnp.concatenate([start] * 4 + [start + size] * 4, axis=0).astype(F32).T.astype(I32)
    start = both[:, 0:1]
    end = both[:, 4:5]
    lane = lax.broadcasted_iota(I32, (group, NOSV), 1)
    code = jnp.zeros((group, NOSV), I32)
    for i in range(4):
        position = lane + i * NOSV
        inside = (position >= start) & (position < end)
        code += jnp.where(inside, domain[:, i * NOSV : (i + 1) * NOSV] + 1, 0)
    code = (code + pltpu.roll(code, CAP, 1) - 1).astype(F32)
    odd = lax.broadcasted_iota(I32, (group, NOSV), 0) % 2 == 1
    code = jnp.where(odd & (code >= 0.0), code + AUXD, code)
    columns[...] = code.T

    lanes = lax.broadcasted_iota(I32, (2 * CAP, 2 * AUXD), 1).astype(F32)
    upper = lax.broadcasted_iota(I32, (2 * CAP, 1), 0) < CAP
    for i in range(PARTS):
        load(i).wait()
        for g in range(i * part, (i + 1) * part, 2):
            column = jnp.where(upper, columns[:, g : g + 1], columns[:, g + 1 : g + 2])
            pick = jnp.where(lanes == column, 1.0, 0.0).astype(BF16)
            pair = rows[g : g + 2].reshape(2 * AUXD, NOSV)
            got = jnp.dot(pick, pair, preferred_element_type=F32).astype(BF16)
            packed[g] = got[:CAP]
            packed[g + 1] = got[CAP:]
        save(i).start()
    for i in range(PARTS):
        save(i).wait()


def pack_rows(where_am_i, domain, counts, raw_rows):
    group = raw_rows.shape[0]
    smem = pl.BlockSpec(memory_space=pltpu.SMEM)
    vmem = pl.BlockSpec(memory_space=pltpu.VMEM)
    hbm = pl.BlockSpec(memory_space=pltpu.HBM)
    return pl.pallas_call(
        pack_kernel,
        in_specs=[smem, vmem, vmem, hbm],
        out_specs=hbm,
        out_shape=pltpu.HBM((group, CAP, NOSV), BF16),
        scratch_shapes=[
            pltpu.VMEM(raw_rows.shape, BF16),
            pltpu.VMEM((group, CAP, NOSV), BF16),
            pltpu.VMEM((NOSV, group), F32),
            pltpu.SemaphoreType.DMA((PARTS,)),
            pltpu.SemaphoreType.DMA((PARTS,)),
        ],
        compiler_params=params(),
        name="pack_rows",
    )(where_am_i, domain, counts, pltpu.with_memory_space_constraint(raw_rows, pltpu.HBM))


def tables_kernel(where_am_i, counts, ids, occ, domain, osv, out, windows, table):
    me = where_am_i[0]
    lane = lax.broadcasted_iota(I32, (1, NOSV), 1)
    energies = osv[...].astype(F32)
    for k in range(OCC):
        row = domain[pl.ds(me * OCC + k, 1), :]
        for i in range(4):
            windows[2 * i : 2 * i + 1, :] = row[:, i * NOSV : (i + 1) * NOSV]
            if i < 3:
                windows[2 * i + 1 : 2 * i + 2, :] = row[:, i * NOSV + CAP : (i + 1) * NOSV + CAP]
        table[...] = jnp.zeros(table.shape, F32)
        starts = jnp.zeros((1, NOSV), I32)
        start = jnp.int32(0)
        for a in range(NAUX_DEV):
            end = start + counts[a, me * OCC + k]
            chunk = jnp.minimum(start // CAP, CHUNKS - 2)
            at = chunk * CAP
            entry = windows[pl.ds(chunk, 1), :]
            entry = jnp.where((lane >= start - at) & (lane < end - at), entry, -1)
            table[a : a + 1, :] = entry.astype(F32)
            starts = jnp.where(lane == a, at, starts)
            start = end
        table[16:17, :] = starts.astype(F32)
        term = energies[k : k + 1, :] - occ[ids[k]]
        for i in range(3):
            rounded = term.astype(BF16).astype(F32)
            table[17 + i : 18 + i, :] = rounded
            term = term - rounded
        out[k] = table[...].astype(BF16)


def slot_tables(where_am_i, counts, ids, occ, domain, osv):
    smem = pl.BlockSpec(memory_space=pltpu.SMEM)
    vmem = pl.BlockSpec(memory_space=pltpu.VMEM)
    return pl.pallas_call(
        tables_kernel,
        in_specs=[smem, smem, smem, smem, vmem, vmem],
        out_specs=vmem,
        out_shape=jax.ShapeDtypeStruct((OCC, TAIL, NOSV), BF16),
        scratch_shapes=[pltpu.VMEM((8, NOSV), I32), pltpu.VMEM((TAIL, NOSV), F32)],
        compiler_params=params(),
        name="slot_tables",
    )(where_am_i, counts, ids, occ, domain, osv)


def fit_kernel(where_am_i, counts, received, metric, tail, fitted, block, acc):
    k = pl.program_id(0)
    acc[...] = jnp.zeros(acc.shape, F32)
    sub = lax.broadcasted_iota(I32, (CAP, NOSV), 0)
    start = jnp.int32(0)
    for a in range(NAUX_DEV):
        at = pl.multiple_of(jnp.minimum(start // CAP, CHUNKS - 1) * CAP, CAP)
        first = start % CAP
        rows = received[a, 0].astype(F32)
        acc[pl.ds(at, CAP), :] += jnp.where(sub >= first, rows, 0.0)
        acc[pl.ds(at + CAP, CAP), :] += jnp.where(sub >= first, 0.0, rows)
        start += counts[a, where_am_i[0] * OCC + k]
    whole = acc[:NFIT, :].astype(BF16)
    block[0] = whole
    fitted[0, :NFIT] = jnp.dot(metric[0], whole, preferred_element_type=F32).astype(BF16)
    fitted[0, NFIT:] = tail[0]


def fit(where_am_i, counts, received, metric, tail):
    def one(shape):
        return pl.BlockSpec((1,) + shape, lambda k, s: (k, 0, 0))

    return pl.pallas_call(
        fit_kernel,
        grid_spec=pltpu.PrefetchScalarGridSpec(
            num_scalar_prefetch=1,
            grid=(OCC,),
            in_specs=[
                pl.BlockSpec(memory_space=pltpu.SMEM),
                pl.BlockSpec((NAUX_DEV, 1, CAP, NOSV), lambda k, s: (0, k, 0, 0)),
                one((NFIT, NFIT)),
                one((TAIL, NOSV)),
            ],
            out_specs=[one((ROWS, NOSV)), one((NFIT, NOSV))],
            scratch_shapes=[pltpu.VMEM((NFIT + CAP, NOSV), F32)],
        ),
        out_shape=[
            jax.ShapeDtypeStruct((OCC, ROWS, NOSV), BF16),
            jax.ShapeDtypeStruct((OCC, NFIT, NOSV), BF16),
        ],
        compiler_params=params(),
        name="fit",
    )(where_am_i, counts, received, metric, tail)


def spread_rows(source, table, starts, at_slot, store):
    sub = lax.broadcasted_iota(I32, (AUXD, 2 * CAP), 0).astype(F32)
    for a in range(NAUX_DEV):
        at = pl.multiple_of(starts[at_slot, a], CAP)
        pick = jnp.where(sub == table[a : a + 1, :], 1.0, 0.0).astype(BF16)
        store(a, jnp.dot(pick, source[pl.ds(at, 2 * CAP), :], preferred_element_type=F32))


def energy_of(tail):
    return tail[1:2, :] + tail[2:3, :] + tail[3:4, :]


def read_starts(sources, starts_v, starts_s, sem):
    for i, source in enumerate(sources):
        starts_v[i : i + 1, :] = source[NFIT + 16 :, :].astype(F32)[0:1, :].astype(I32)
    copy = pltpu.make_async_copy(starts_v, starts_s, sem)
    copy.start()
    copy.wait()


def own_columns(tails):
    rows = [energy_of(t) for t in tails]
    return jnp.concatenate(rows + rows, axis=0).T


def one_round(
    q, slot_of, starts, at_slot, screening, columns, raw_t, spread, ints, amps, energy, accumulate
):
    terms = []
    for l in range(OCC):

        def store(a, value, l=l):
            spread[a * AUXD : (a + 1) * AUXD, l * NOSV : (l + 1) * NOSV] = value.astype(BF16)

        source = slot_of(l)
        tail = source[NFIT:, :].astype(F32)
        terms.append(energy_of(tail[16:, :]))
        spread_rows(source, tail, starts, at_slot + l, store)
    ints[...] = jnp.dot(raw_t[...], spread[...], preferred_element_type=F32)
    for k in range(OCC):
        for l in range(OCC):
            ks = slice(k * NOSV, (k + 1) * NOSV)
            ls = slice(l * NOSV, (l + 1) * NOSV)
            value = ints[ks, ls]
            denominator = columns[:, k : k + 1] + terms[l]
            amp = (screening[k, q, l].astype(F32) * value / denominator).astype(BF16)
            amps[ks, ls] = amp
            part = jnp.sum(amp.astype(F32) * value, axis=0, keepdims=True)
            energy[q, k * OCC + l : k * OCC + l + 1, :] = part
    for m in range(NAUX // TILE):
        rows = spread[m * TILE : (m + 1) * TILE, :]
        accumulate(
            m,
            lax.dot_general(
                rows, amps[...], (((1,), (1,)), ((), ())), preferred_element_type=F32
            ),
        )


def own_kernel(
    screening, fitted, block, raw_out, den, energy,
    starts_v, starts_s, spread, ints, amps, sem,
):
    read_starts([fitted.at[k] for k in range(OCC)], starts_v, starts_s, sem.at[0])
    for k in range(OCC):

        def store(a, value, k=k):
            raw_out[k * NOSV : (k + 1) * NOSV, a * AUXD : (a + 1) * AUXD] = value.T.astype(BF16)

        spread_rows(block.at[k], fitted[k, NFIT:, :].astype(F32), starts_s, k, store)
    energy[...] = jnp.zeros(energy.shape, F32)
    columns = own_columns([fitted[k, NFIT + 16 :, :].astype(F32) for k in range(OCC)])

    def accumulate(m, value):
        den[m * TILE : (m + 1) * TILE, :] = value

    one_round(
        0, lambda l: fitted.at[l], starts_s, 0, screening, columns, raw_out, spread, ints, amps, energy, accumulate
    )


def round_scratch():
    return [
        pltpu.VMEM((NAUX, SLAB), BF16),
        pltpu.VMEM((SLAB, SLAB), F32),
        pltpu.VMEM((SLAB, SLAB), BF16),
    ]


def own_round(screening, fitted, block):
    smem = pl.BlockSpec(memory_space=pltpu.SMEM)
    vmem = pl.BlockSpec(memory_space=pltpu.VMEM)
    return pl.pallas_call(
        own_kernel,
        in_specs=[smem, vmem, vmem],
        out_specs=[vmem, vmem, vmem],
        out_shape=[
            jax.ShapeDtypeStruct((SLAB, NAUX), BF16),
            pltpu.VMEM((NAUX, SLAB), F32),
            jax.ShapeDtypeStruct((5, 16, NOSV), F32),
        ],
        scratch_shapes=[
            pltpu.VMEM((8, NOSV), I32),
            pltpu.SMEM((8, NOSV), I32),
        ]
        + round_scratch()
        + [pltpu.SemaphoreType.DMA((1,))],
        compiler_params=params(),
        name="own_round",
    )(screening, fitted, block)


def phase_kernel(masks, last, pieces, matchings, screening, own_tail, raw_t, den_in, *rest):
    far = rest[: len(pieces)]
    rest = rest[len(pieces) :]
    den, energy = rest[:2]
    rest = rest[2:]
    if last:
        den_out = rest[0]
        rest = rest[1:]
    source, starts_v, starts_s, spread, ints, amps, piece_sems, sem = rest[:8]

    def wanted(mask):
        found = mask == masks[0]
        for other in masks[1:]:
            found |= mask == other
        return found

    count = wanted(matchings[0, 0]).astype(I32)
    for q in range(1, 4):
        count += wanted(matchings[q, 0]).astype(I32)
    energy[...] = jnp.zeros(energy.shape, F32)

    def fetch(index):
        mask, lo, hi = pieces[index]
        target = source.at[masks.index(mask), pl.ds(lo, hi - lo)]
        return pltpu.make_async_copy(far[index], target, piece_sems.at[index])

    def accumulate(m, value):
        rows = pl.ds(m * TILE, TILE)
        den[rows, :] = den[rows, :] + value

    @pl.when(count > 0)
    def _():
        for index in range(len(pieces)):
            fetch(index).start()
        for index in range(len(pieces)):
            fetch(index).wait()
        slots = [source.at[i, l] for i in range(len(masks)) for l in range(OCC)]
        read_starts(slots, starts_v, starts_s, sem.at[0])
        columns = own_columns([own_tail[k, 16:, :].astype(F32) for k in range(OCC)])

        def body(q, carry):
            mask = matchings[q, 0]

            @pl.when(wanted(mask))
            def _():
                which = jnp.int32(0)
                for i in range(1, len(masks)):
                    which = jnp.where(mask == masks[i], i, which)
                one_round(
                    q + 1, lambda l: source.at[which, l], starts_s, which * OCC, screening, columns,
                    raw_t, spread, ints, amps, energy, accumulate,
                )

            return carry

        lax.fori_loop(0, 4, body, 0)

    if last:
        short, sems = rest[8:]
        tiles = NAUX // TILE
        each = NAUX_DEV // tiles
        sends = []
        for m in range(tiles):
            for a in range(m * each, (m + 1) * each):
                for k in range(OCC):
                    short[a, k] = den[a * AUXD : (a + 1) * AUXD, k * NOSV : (k + 1) * NOSV].astype(BF16)
            owners = pl.ds(m * each, each)
            send = pltpu.make_async_copy(short.at[owners], den_out.at[owners], sems.at[m])
            send.start()
            sends.append(send)
        for send in sends:
            send.wait()


def phase(masks, last, pieces, matchings, screening, own_tail, raw_t, den, far):
    smem = pl.BlockSpec(memory_space=pltpu.SMEM)
    vmem = pl.BlockSpec(memory_space=pltpu.VMEM)
    hbm = pl.BlockSpec(memory_space=pl.ANY)
    out_specs = [vmem, vmem]
    out_shape = [pltpu.VMEM((NAUX, SLAB), F32), jax.ShapeDtypeStruct((5, 16, NOSV), F32)]
    more = []
    if last:
        sent = (NAUX_DEV, OCC, AUXD, NOSV)
        out_specs.append(hbm)
        out_shape.append(pltpu.HBM(sent, BF16))
        more = [pltpu.VMEM(sent, BF16), pltpu.SemaphoreType.DMA((NAUX // TILE,))]
    rows = -(-len(masks) * OCC // 8) * 8
    return pl.pallas_call(
        functools.partial(phase_kernel, masks, last, pieces),
        in_specs=[smem, smem, vmem, vmem, vmem] + [hbm] * len(far),
        out_specs=out_specs,
        out_shape=out_shape,
        scratch_shapes=[
            pltpu.VMEM((len(masks), OCC, ROWS, NOSV), BF16),
            pltpu.VMEM((rows, NOSV), I32),
            pltpu.SMEM((rows, NOSV), I32),
        ]
        + round_scratch()
        + [pltpu.SemaphoreType.DMA((len(pieces),)), pltpu.SemaphoreType.DMA((1,))]
        + more,
        input_output_aliases={4: 0},
        compiler_params=params(),
        name="phase_" + "_".join(str(m) for m in masks),
    )(matchings, screening, own_tail, raw_t, pltpu.with_memory_space_constraint(den, pltpu.VMEM), *far)


def widen_kernel(short, wide):
    wide[...] = short[...].astype(F32)


def widen(short):
    blocks = 4
    spec = pl.BlockSpec((short.shape[0] // blocks,) + short.shape[1:], lambda i: (i, 0, 0))
    return pl.pallas_call(
        widen_kernel,
        grid=(blocks,),
        in_specs=[spec],
        out_specs=spec,
        out_shape=jax.ShapeDtypeStruct(short.shape, F32),
        compiler_params=params(),
        name="widen",
    )(short)


def flip(x, mask):
    return lax.ppermute(x, "orb", [(i, i ^ mask) for i in range(lax.axis_size("orb"))])


def per_device(
    raw_rows, fit_metric, domain, counts, orbital_ids, occ_energy, osv_energy, matchings, screening
):
    where_am_i = lax.axis_index("aux").astype(I32).reshape(1)
    group = raw_rows.shape[0]
    counts = counts.T
    packed = pack_rows(where_am_i, domain, counts, raw_rows)
    packed = packed.reshape(NAUX_DEV, OCC, CAP, NOSV)
    received = lax.all_to_all(packed, "aux", split_axis=0, concat_axis=0, tiled=True)
    tail = slot_tables(where_am_i, counts, orbital_ids, occ_energy, domain, osv_energy)
    fitted, block = fit(where_am_i, counts, received, fit_metric, tail)

    near = (flip(fitted, 1), flip(fitted, 2), flip(fitted, 6))
    raw_t, den, energy0 = own_round(screening, fitted, block)
    near, den = lax.optimization_barrier((near, den))
    far1, far2, far6 = near
    middle = (flip(far2, 1), flip(far6, 2), flip(far1, 6))
    common = (matchings, screening, tail, raw_t)
    den, energy1 = phase((1, 2, 6), False, ((1, 0, 4), (2, 0, 4), (6, 0, 4)), *common, den, near)
    middle, den = lax.optimization_barrier((middle, den))
    far3, far4, far7 = middle
    far5 = (flip(far4[0:1], 1), flip(far7[1:2], 2), flip(far3[2:4], 6))
    den, energy2 = phase((3, 4, 7), False, ((3, 0, 4), (4, 0, 4), (7, 0, 4)), *common, den, middle)
    _, energy3, sent = phase((5,), True, ((5, 0, 1), (5, 1, 2), (5, 2, 4)), *common, den, far5)
    returned = lax.all_to_all(sent, "aux", split_axis=0, concat_axis=0, tiled=True)
    density = widen(returned.reshape(group, AUXD, NOSV))
    total = jnp.sum(energy0 + energy1 + energy2 + energy3, axis=2)
    energies = total.reshape(5, OCC, OCC).transpose(1, 0, 2) * (PAIR_SCALE / (NOSV * NOSV))
    return density, energies


def solution(mesh):
    placed = (
        P("orb", "aux", None),
        P(("orb", "aux"), None, None),
        P("orb", None),
        P("orb", None),
        P(("orb", "aux")),
        P(),
        P(("orb", "aux"), None),
        P(),
        P(("orb", "aux"), None, None),
    )
    return jax.shard_map(
        per_device,
        mesh=mesh,
        in_specs=placed,
        out_specs=(P("orb", "aux", None), P(("orb", "aux"), None, None)),
        check_vma=False,
    )
```

```python
import functools

import jax
import jax.numpy as jnp
from jax import lax
from jax.experimental import pallas as pl
from jax.experimental.pallas import tpu as pltpu
from jax.sharding import PartitionSpec as P

PAIR_SCALE = 1.3
BF16 = jnp.bfloat16
F32 = jnp.float32
I32 = jnp.int32
NOSV = 128
NFIT = 512
OCC = 4
AUXD = 128
NAUX_DEV = 16
NAUX = AUXD * NAUX_DEV
CAP = 64
CHUNKS = NFIT // CAP
TAIL = 32
ROWS = NFIT + TAIL
TILE = 512
PARTS = 4
SLAB = OCC * NOSV
VMEM_LIMIT = 28 * 1024 * 1024


def params(**kw):
    return pltpu.CompilerParams(vmem_limit_bytes=VMEM_LIMIT, **kw)


def pack_kernel(
    where_am_i, domain_in, counts_in, raw, out, domain, counts, rows, packed, columns, in_sems, out_sems, sems
):
    group = raw.shape[0]
    part = group // PARTS

    def load(i):
        span = pl.ds(i * part, part)
        return pltpu.make_async_copy(raw.at[span], rows.at[span], in_sems.at[i])

    def save(i):
        span = pl.ds(i * part, part)
        return pltpu.make_async_copy(packed.at[span], out.at[span], out_sems.at[i])

    small = (
        pltpu.make_async_copy(counts_in, counts, sems.at[0]),
        pltpu.make_async_copy(domain_in, domain, sems.at[1]),
    )
    for copy in small:
        copy.start()
    for i in range(PARTS):
        load(i).start()
    for copy in small:
        copy.wait()
    me = where_am_i[0]
    owner = lax.broadcasted_iota(I32, (NAUX_DEV, group), 0)
    start = jnp.sum(jnp.where(owner < me, counts[...], 0), axis=0, keepdims=True)
    size = jnp.sum(jnp.where(owner == me, counts[...], 0), axis=0, keepdims=True)
    both = jnp.concatenate([start] * 4 + [start + size] * 4, axis=0).astype(F32).T.astype(I32)
    start = both[:, 0:1]
    end = both[:, 4:5]
    lane = lax.broadcasted_iota(I32, (group, NOSV), 1)
    code = jnp.zeros((group, NOSV), I32)
    for i in range(4):
        position = lane + i * NOSV
        inside = (position >= start) & (position < end)
        code += jnp.where(inside, domain[:, i * NOSV : (i + 1) * NOSV] + 1, 0)
    code = (code + pltpu.roll(code, CAP, 1) - 1).astype(F32)
    columns[...] = code.T

    lanes = lax.broadcasted_iota(I32, (CAP, AUXD), 1).astype(F32)
    for i in range(PARTS):
        load(i).wait()
        for g in range(i * part, (i + 1) * part):
            pick = jnp.where(lanes == columns[:CAP, g : g + 1], 1.0, 0.0).astype(BF16)
            packed[g] = jnp.dot(pick, rows[g], preferred_element_type=F32).astype(BF16)
        save(i).start()
    for i in range(PARTS):
        save(i).wait()


def pack_rows(where_am_i, domain, counts, raw_rows):
    group = raw_rows.shape[0]
    smem = pl.BlockSpec(memory_space=pltpu.SMEM)
    hbm = pl.BlockSpec(memory_space=pltpu.HBM)
    return pl.pallas_call(
        pack_kernel,
        in_specs=[smem, hbm, hbm, hbm],
        out_specs=hbm,
        out_shape=pltpu.HBM((group, CAP, NOSV), BF16),
        scratch_shapes=[
            pltpu.VMEM(domain.shape, I32),
            pltpu.VMEM(counts.shape, I32),
            pltpu.VMEM(raw_rows.shape, BF16),
            pltpu.VMEM((group, CAP, NOSV), BF16),
            pltpu.VMEM((NOSV, group), F32),
            pltpu.SemaphoreType.DMA((PARTS,)),
            pltpu.SemaphoreType.DMA((PARTS,)),
            pltpu.SemaphoreType.DMA((2,)),
        ],
        compiler_params=params(),
        name="pack_rows",
    )(where_am_i, *(pltpu.with_memory_space_constraint(x, pltpu.HBM) for x in (domain, counts, raw_rows)))


def tables_kernel(where_am_i, counts, ids, occ, domain, osv, out, windows, table):
    me = where_am_i[0]
    lane = lax.broadcasted_iota(I32, (1, NOSV), 1)
    energies = osv[...].astype(F32)
    for k in range(OCC):
        row = domain[pl.ds(me * OCC + k, 1), :]
        for i in range(4):
            windows[2 * i : 2 * i + 1, :] = row[:, i * NOSV : (i + 1) * NOSV]
            if i < 3:
                windows[2 * i + 1 : 2 * i + 2, :] = row[:, i * NOSV + CAP : (i + 1) * NOSV + CAP]
        table[...] = jnp.zeros(table.shape, F32)
        starts = jnp.zeros((1, NOSV), I32)
        start = jnp.int32(0)
        for a in range(NAUX_DEV):
            end = start + counts[a, me * OCC + k]
            chunk = jnp.minimum(start // CAP, CHUNKS - 2)
            at = chunk * CAP
            entry = windows[pl.ds(chunk, 1), :]
            entry = jnp.where((lane >= start - at) & (lane < end - at), entry, -1)
            table[a : a + 1, :] = entry.astype(F32)
            starts = jnp.where(lane == a, at, starts)
            start = end
        table[16:17, :] = starts.astype(F32)
        term = energies[k : k + 1, :] - occ[ids[k]]
        for i in range(3):
            rounded = term.astype(BF16).astype(F32)
            table[17 + i : 18 + i, :] = rounded
            term = term - rounded
        out[k] = table[...].astype(BF16)


def slot_tables(where_am_i, counts, ids, occ, domain, osv):
    smem = pl.BlockSpec(memory_space=pltpu.SMEM)
    vmem = pl.BlockSpec(memory_space=pltpu.VMEM)
    return pl.pallas_call(
        tables_kernel,
        in_specs=[smem, smem, smem, smem, vmem, vmem],
        out_specs=vmem,
        out_shape=jax.ShapeDtypeStruct((OCC, TAIL, NOSV), BF16),
        scratch_shapes=[pltpu.VMEM((8, NOSV), I32), pltpu.VMEM((TAIL, NOSV), F32)],
        compiler_params=params(),
        name="slot_tables",
    )(where_am_i, counts, ids, occ, domain, osv)


def fit_kernel(where_am_i, counts, received, metric, tail, fitted, block, acc, whole, sems):
    sub = lax.broadcasted_iota(I32, (CAP, NOSV), 0)
    starts = [jnp.int32(0)] * OCC
    for a in range(NAUX_DEV):
        for k in range(OCC):
            at = pl.multiple_of(jnp.minimum(starts[k] // CAP, CHUNKS - 1) * CAP, CAP)
            here = sub >= starts[k] % CAP
            rows = received[a, k].astype(F32)
            pltpu.store(acc.at[k, pl.ds(at, CAP), :], rows, mask=here)
            pltpu.store(acc.at[k, pl.ds(at + CAP, CAP), :], rows, mask=jnp.logical_not(here))
            starts[k] += counts[a, where_am_i[0] * OCC + k]
    saves = [pltpu.make_async_copy(whole.at[k], block.at[k], sems.at[k]) for k in range(OCC)]
    for k in range(OCC):
        whole[k] = acc[k, :NFIT, :].astype(BF16)
        saves[k].start()
        fitted[k, :NFIT] = jnp.dot(metric[k], whole[k], preferred_element_type=F32).astype(BF16)
        fitted[k, NFIT:] = tail[k]
    for save in saves:
        save.wait()


def fit(where_am_i, counts, received, metric, tail):
    smem = pl.BlockSpec(memory_space=pltpu.SMEM)
    vmem = pl.BlockSpec(memory_space=pltpu.VMEM)
    return pl.pallas_call(
        fit_kernel,
        in_specs=[smem, smem, vmem, vmem, vmem],
        out_specs=[vmem, pl.BlockSpec(memory_space=pltpu.HBM)],
        out_shape=[jax.ShapeDtypeStruct((OCC, ROWS, NOSV), BF16), pltpu.HBM((OCC, NFIT, NOSV), BF16)],
        scratch_shapes=[
            pltpu.VMEM((OCC, NFIT + CAP, NOSV), F32),
            pltpu.VMEM((OCC, NFIT, NOSV), BF16),
            pltpu.SemaphoreType.DMA((OCC,)),
        ],
        compiler_params=params(),
        name="fit",
    )(where_am_i, counts, received, metric, tail)


def spread_rows(source, table, starts, at_slot, store):
    sub = lax.broadcasted_iota(I32, (AUXD, 2 * CAP), 0).astype(F32)
    for a in range(NAUX_DEV):
        at = pl.multiple_of(starts[at_slot, a], CAP)
        pick = jnp.where(sub == table[a : a + 1, :], 1.0, 0.0).astype(BF16)
        store(a, jnp.dot(pick, source[pl.ds(at, 2 * CAP), :], preferred_element_type=F32))


def energy_of(tail):
    return tail[1:2, :] + tail[2:3, :] + tail[3:4, :]


def read_starts(sources, starts_v, starts_s, sem):
    for i, source in enumerate(sources):
        starts_v[i : i + 1, :] = source[NFIT + 16 :, :].astype(F32)[0:1, :].astype(I32)
    copy = pltpu.make_async_copy(starts_v, starts_s, sem)
    copy.start()
    copy.wait()


def own_columns(tails):
    rows = [energy_of(t) for t in tails]
    return jnp.concatenate(rows + rows, axis=0).T


def one_round(
    q, slot_of, starts, at_slot, screening, columns, raw_t, spread, ints, amps, energy, density
):
    terms = []
    for l in range(OCC):

        def store(a, value, l=l):
            spread[a * AUXD : (a + 1) * AUXD, l * NOSV : (l + 1) * NOSV] = value.astype(BF16)

        source = slot_of(l)
        tail = source[NFIT:, :].astype(F32)
        terms.append(energy_of(tail[16:, :]))
        spread_rows(source, tail, starts, at_slot + l, store)
    ints[...] = jnp.dot(raw_t[...], spread[...], preferred_element_type=F32)
    for k in range(OCC):
        for l in range(OCC):
            ks = slice(k * NOSV, (k + 1) * NOSV)
            ls = slice(l * NOSV, (l + 1) * NOSV)
            value = ints[ks, ls]
            denominator = columns[:, k : k + 1] + terms[l]
            amp = (screening[k, q, l].astype(F32) * value / denominator).astype(BF16)
            amps[ks, ls] = amp
            part = jnp.sum(amp.astype(F32) * value, axis=0, keepdims=True)
            energy[q, k * OCC + l : k * OCC + l + 1, :] = part

    def add_to(before, after):
        for m in range(NAUX // TILE):
            ms = slice(m * TILE, (m + 1) * TILE)
            value = lax.dot_general(
                spread[ms, :], amps[...], (((1,), (1,)), ((), ())), preferred_element_type=F32
            )
            after[ms, :] = value if before is None else before[ms, :] + value

    density(add_to)


def own_kernel(
    screening, fitted, block_in, raw_out, den, energy,
    block, starts_v, starts_s, spread, ints, amps, sem,
):
    load = pltpu.make_async_copy(block_in, block, sem.at[1])
    load.start()
    read_starts([fitted.at[k] for k in range(OCC)], starts_v, starts_s, sem.at[0])
    load.wait()
    for k in range(OCC):

        def store(a, value, k=k):
            raw_out[k * NOSV : (k + 1) * NOSV, a * AUXD : (a + 1) * AUXD] = value.T.astype(BF16)

        spread_rows(block.at[k], fitted[k, NFIT:, :].astype(F32), starts_s, k, store)
    energy[...] = jnp.zeros(energy.shape, F32)
    columns = own_columns([fitted[k, NFIT + 16 :, :].astype(F32) for k in range(OCC)])

    one_round(
        0, lambda l: fitted.at[l], starts_s, 0, screening, columns, raw_out, spread, ints, amps, energy,
        lambda add_to: add_to(None, den),
    )


def round_scratch():
    return [
        pltpu.VMEM((NAUX, SLAB), BF16),
        pltpu.VMEM((SLAB, SLAB), F32),
        pltpu.VMEM((SLAB, SLAB), BF16),
    ]


def own_round(screening, fitted, block):
    smem = pl.BlockSpec(memory_space=pltpu.SMEM)
    vmem = pl.BlockSpec(memory_space=pltpu.VMEM)
    return pl.pallas_call(
        own_kernel,
        in_specs=[smem, vmem, pl.BlockSpec(memory_space=pltpu.HBM)],
        out_specs=[vmem, vmem, vmem],
        out_shape=[
            jax.ShapeDtypeStruct((SLAB, NAUX), BF16),
            pltpu.VMEM((NAUX, SLAB), F32),
            jax.ShapeDtypeStruct((5, 16, NOSV), F32),
        ],
        scratch_shapes=[
            pltpu.VMEM(block.shape, BF16),
            pltpu.VMEM((8, NOSV), I32),
            pltpu.SMEM((8, NOSV), I32),
        ]
        + round_scratch()
        + [pltpu.SemaphoreType.DMA((2,))],
        compiler_params=params(),
        name="own_round",
    )(screening, fitted, pltpu.with_memory_space_constraint(block, pltpu.HBM))


def phase_kernel(masks, last, pieces, matchings, screening, own_tail, raw_t, den_in, *rest):
    far = rest[: len(pieces)]
    rest = rest[len(pieces) :]
    if last:
        energy, den_out, source, starts_v, starts_s, spread, ints, amps, piece_sems, sem, den, short, sems = rest
    else:
        den, energy, source, starts_v, starts_s, spread, ints, amps, piece_sems, sem = rest

    def wanted(mask):
        found = mask == masks[0]
        for other in masks[1:]:
            found |= mask == other
        return found

    count = wanted(matchings[0, 0]).astype(I32)
    for q in range(1, 4):
        count += wanted(matchings[q, 0]).astype(I32)
    energy[...] = jnp.zeros(energy.shape, F32)

    def fetch(index):
        mask, lo, hi = pieces[index]
        target = source.at[masks.index(mask), pl.ds(lo, hi - lo)]
        return pltpu.make_async_copy(far[index], target, piece_sems.at[index])

    def send(final):
        tiles = NAUX // TILE
        each = NAUX_DEV // tiles
        sends = []
        for m in range(tiles):
            for a in range(m * each, (m + 1) * each):
                for k in range(OCC):
                    part = final[a * AUXD : (a + 1) * AUXD, k * NOSV : (k + 1) * NOSV]
                    short[a, k] = part.astype(BF16)
            owners = pl.ds(m * each, each)
            copy = pltpu.make_async_copy(short.at[owners], den_out.at[owners], sems.at[m])
            copy.start()
            sends.append(copy)
        for copy in sends:
            copy.wait()

    @pl.when(count > 0)
    def _():
        for index in range(len(pieces)):
            fetch(index).start()
        for index in range(len(pieces)):
            fetch(index).wait()
        slots = [source.at[i, l] for i in range(len(masks)) for l in range(OCC)]
        read_starts(slots, starts_v, starts_s, sem.at[0])
        columns = own_columns([own_tail[k, 16:, :].astype(F32) for k in range(OCC)])

        def body(q, done):
            mask = matchings[q, 0]

            def density(add_to):
                @pl.when(done == 0)
                def _():
                    add_to(den_in, den)

                @pl.when(done > 0)
                def _():
                    add_to(den, den)

            @pl.when(wanted(mask))
            def _():
                which = jnp.int32(0)
                for i in range(1, len(masks)):
                    which = jnp.where(mask == masks[i], i, which)
                one_round(
                    q + 1, lambda l: source.at[which, l], starts_s, which * OCC, screening, columns,
                    raw_t, spread, ints, amps, energy, density,
                )

            return done + wanted(mask).astype(I32)

        lax.fori_loop(0, 4, body, jnp.int32(0))
        if last:
            send(den)

    @pl.when(count == 0)
    def _():
        if last:
            send(den_in)
        else:
            den[...] = den_in[...]


def phase(masks, last, pieces, matchings, screening, own_tail, raw_t, den, far):
    smem = pl.BlockSpec(memory_space=pltpu.SMEM)
    vmem = pl.BlockSpec(memory_space=pltpu.VMEM)
    hbm = pl.BlockSpec(memory_space=pl.ANY)
    energy = jax.ShapeDtypeStruct((5, 16, NOSV), F32)
    if last:
        sent = (NAUX_DEV, OCC, AUXD, NOSV)
        out_specs = [vmem, hbm]
        out_shape = [energy, pltpu.HBM(sent, BF16)]
        more = [
            pltpu.VMEM((NAUX, SLAB), F32),
            pltpu.VMEM(sent, BF16),
            pltpu.SemaphoreType.DMA((NAUX // TILE,)),
        ]
        alias = {}
    else:
        out_specs = [vmem, vmem]
        out_shape = [pltpu.VMEM((NAUX, SLAB), F32), energy]
        more = []
        alias = {4: 0}
    rows = -(-len(masks) * OCC // 8) * 8
    return pl.pallas_call(
        functools.partial(phase_kernel, masks, last, pieces),
        in_specs=[smem, smem, vmem, vmem, vmem] + [hbm] * len(far),
        out_specs=out_specs,
        out_shape=out_shape,
        scratch_shapes=[
            pltpu.VMEM((len(masks), OCC, ROWS, NOSV), BF16),
            pltpu.VMEM((rows, NOSV), I32),
            pltpu.SMEM((rows, NOSV), I32),
        ]
        + round_scratch()
        + [pltpu.SemaphoreType.DMA((len(pieces),)), pltpu.SemaphoreType.DMA((1,))]
        + more,
        input_output_aliases=alias,
        compiler_params=params(),
        name="phase_" + "_".join(str(m) for m in masks),
    )(matchings, screening, own_tail, raw_t, pltpu.with_memory_space_constraint(den, pltpu.VMEM), *far)


def widen_kernel(short, wide):
    wide[...] = short[...].astype(F32)


def widen(short):
    blocks = 4
    spec = pl.BlockSpec((short.shape[0] // blocks,) + short.shape[1:], lambda i: (i, 0, 0))
    return pl.pallas_call(
        widen_kernel,
        grid=(blocks,),
        in_specs=[spec],
        out_specs=spec,
        out_shape=jax.ShapeDtypeStruct(short.shape, F32),
        compiler_params=params(),
        name="widen",
    )(short)


def flip(x, mask):
    return lax.ppermute(x, "orb", [(i, i ^ mask) for i in range(lax.axis_size("orb"))])


def per_device(
    raw_rows, fit_metric, domain, counts, orbital_ids, occ_energy, osv_energy, matchings, screening
):
    where_am_i = lax.axis_index("aux").astype(I32).reshape(1)
    group = raw_rows.shape[0]
    counts = counts.T
    packed = pack_rows(where_am_i, domain, counts, raw_rows)
    packed = packed.reshape(NAUX_DEV, OCC, CAP, NOSV)
    received = lax.all_to_all(packed, "aux", split_axis=0, concat_axis=0, tiled=True)
    tail = slot_tables(where_am_i, counts, orbital_ids, occ_energy, domain, osv_energy)
    fitted, block = fit(where_am_i, counts, received, fit_metric, tail)

    near = (flip(fitted, 1), flip(fitted, 2), flip(fitted, 6))
    raw_t, den, energy0 = own_round(screening, fitted, block)
    near, den = lax.optimization_barrier((near, den))
    far1, far2, far6 = near
    middle = (flip(far2, 1), flip(far6, 2), flip(far1, 6))
    common = (matchings, screening, tail, raw_t)
    den, energy1 = phase((1, 2, 6), False, ((1, 0, 4), (2, 0, 4), (6, 0, 4)), *common, den, near)
    middle, den = lax.optimization_barrier((middle, den))
    far3, far4, far7 = middle
    far5 = (flip(far4[0:1], 1), flip(far7[1:2], 2), flip(far3[2:4], 6))
    den, energy2 = phase((3, 4, 7), False, ((3, 0, 4), (4, 0, 4), (7, 0, 4)), *common, den, middle)
    energy3, sent = phase((5,), True, ((5, 0, 1), (5, 1, 2), (5, 2, 4)), *common, den, far5)
    returned = lax.all_to_all(sent, "aux", split_axis=0, concat_axis=0, tiled=True)
    density = widen(returned.reshape(group, AUXD, NOSV))
    total = jnp.sum(energy0 + energy1 + energy2 + energy3, axis=2)
    energies = total.reshape(5, OCC, OCC).transpose(1, 0, 2) * (PAIR_SCALE / (NOSV * NOSV))
    return density, energies


def solution(mesh):
    placed = (
        P("orb", "aux", None),
        P(("orb", "aux"), None, None),
        P("orb", None),
        P("orb", None),
        P(("orb", "aux")),
        P(),
        P(("orb", "aux"), None),
        P(),
        P(("orb", "aux"), None, None),
    )
    return jax.shard_map(
        per_device,
        mesh=mesh,
        in_specs=placed,
        out_specs=(P("orb", "aux", None), P(("orb", "aux"), None, None)),
        check_vma=False,
    )
```

```python
import functools

import jax
import jax.numpy as jnp
from jax import lax
from jax.experimental import pallas as pl
from jax.experimental.pallas import tpu as pltpu
from jax.sharding import PartitionSpec as P

PAIR_SCALE = 1.3
BF16 = jnp.bfloat16
F32 = jnp.float32
I32 = jnp.int32
NOSV = 128
NFIT = 512
OCC = 4
AUXD = 128
NAUX_DEV = 16
NAUX = AUXD * NAUX_DEV
CAP = 64
CHUNKS = NFIT // CAP
TAIL = 16
ROWS = NFIT + TAIL
TILE = 512
PARTS = 4
WIDEN_PARTS = 8
SLAB = OCC * NOSV
VMEM_LIMIT = 28 * 1024 * 1024


def params(**kw):
    return pltpu.CompilerParams(vmem_limit_bytes=VMEM_LIMIT, **kw)


def pack_kernel(
    where_am_i, domain_in, counts_in, raw, out, domain, counts, rows, packed, columns, in_sems, out_sems, sems
):
    group = raw.shape[0]
    part = group // PARTS

    def load(i):
        span = pl.ds(i * part, part)
        return pltpu.make_async_copy(raw.at[span], rows.at[span], in_sems.at[i])

    def save(i):
        span = pl.ds(i * part, part)
        return pltpu.make_async_copy(packed.at[span], out.at[span], out_sems.at[i])

    small = (
        pltpu.make_async_copy(counts_in, counts, sems.at[0]),
        pltpu.make_async_copy(domain_in, domain, sems.at[1]),
    )
    for copy in small:
        copy.start()
    for i in range(PARTS):
        load(i).start()
    for copy in small:
        copy.wait()
    me = where_am_i[0]
    owner = lax.broadcasted_iota(I32, (NAUX_DEV, group), 0)
    start = jnp.sum(jnp.where(owner < me, counts[...], 0), axis=0, keepdims=True)
    size = jnp.sum(jnp.where(owner == me, counts[...], 0), axis=0, keepdims=True)
    both = jnp.concatenate([start] * 4 + [start + size] * 4, axis=0).astype(F32).T.astype(I32)
    start = both[:, 0:1]
    end = both[:, 4:5]
    lane = lax.broadcasted_iota(I32, (group, NOSV), 1)
    code = jnp.zeros((group, NOSV), I32)
    for i in range(4):
        position = lane + i * NOSV
        inside = (position >= start) & (position < end)
        code += jnp.where(inside, domain[:, i * NOSV : (i + 1) * NOSV] + 1, 0)
    code = (code + pltpu.roll(code, CAP, 1) - 1).astype(F32)
    columns[...] = code.T

    lanes = lax.broadcasted_iota(I32, (CAP, AUXD), 1).astype(F32)
    for i in range(PARTS):
        load(i).wait()
        for g in range(i * part, (i + 1) * part):
            pick = jnp.where(lanes == columns[:CAP, g : g + 1], 1.0, 0.0).astype(BF16)
            packed[g] = jnp.dot(pick, rows[g], preferred_element_type=F32).astype(BF16)
        save(i).start()
    for i in range(PARTS):
        save(i).wait()


def pack_rows(where_am_i, domain, counts, raw_rows):
    group = raw_rows.shape[0]
    smem = pl.BlockSpec(memory_space=pltpu.SMEM)
    hbm = pl.BlockSpec(memory_space=pltpu.HBM)
    return pl.pallas_call(
        pack_kernel,
        in_specs=[smem, hbm, hbm, hbm],
        out_specs=hbm,
        out_shape=pltpu.HBM((group, CAP, NOSV), BF16),
        scratch_shapes=[
            pltpu.VMEM(domain.shape, I32),
            pltpu.VMEM(counts.shape, I32),
            pltpu.VMEM(raw_rows.shape, BF16),
            pltpu.VMEM((group, CAP, NOSV), BF16),
            pltpu.VMEM((NOSV, group), F32),
            pltpu.SemaphoreType.DMA((PARTS,)),
            pltpu.SemaphoreType.DMA((PARTS,)),
            pltpu.SemaphoreType.DMA((2,)),
        ],
        compiler_params=params(),
        name="pack_rows",
    )(where_am_i, *(pltpu.with_memory_space_constraint(x, pltpu.HBM) for x in (domain, counts, raw_rows)))


def tables_kernel(where_am_i, counts, ids, occ, domain, osv, out, windows, table):
    me = where_am_i[0]
    lane = lax.broadcasted_iota(I32, (1, NOSV), 1)
    energies = osv[...].astype(F32)
    for k in range(OCC):
        row = domain[pl.ds(me * OCC + k, 1), :]
        for i in range(4):
            windows[2 * i : 2 * i + 1, :] = row[:, i * NOSV : (i + 1) * NOSV]
            if i < 3:
                windows[2 * i + 1 : 2 * i + 2, :] = row[:, i * NOSV + CAP : (i + 1) * NOSV + CAP]
        table[...] = jnp.zeros(table.shape, F32)
        firsts = jnp.zeros((1, NOSV), I32)
        behind = jnp.zeros((1, NOSV), I32)
        start = jnp.int32(0)
        for a in range(NAUX_DEV):
            end = start + counts[a, me * OCC + k]
            chunk = jnp.minimum(start // CAP, CHUNKS - 2)
            at = chunk * CAP
            entry = windows[pl.ds(chunk, 1), :]
            entry = jnp.where((lane >= start - at) & (lane < end - at), entry, -1)
            table[a : a + 1, :] = entry.astype(F32)
            firsts = jnp.where(lane == a, at, firsts)
            behind = jnp.where(lane == a, start - at, behind)
            start = end
        wide = jnp.maximum(table[...], pltpu.roll(table[...], CAP, 1))
        table[0:8, :] = jnp.where(lane < CAP, wide[0:8], wide[8:16])
        table[8:16, :] = jnp.zeros((8, NOSV), F32)
        table[8:9, :] = firsts.astype(F32)
        table[9:10, :] = behind.astype(F32)
        term = energies[k : k + 1, :] - occ[ids[k]]
        for i in range(3):
            rounded = term.astype(BF16).astype(F32)
            table[10 + i : 11 + i, :] = rounded
            term = term - rounded
        out[k] = table[...].astype(BF16)


def slot_tables(where_am_i, counts, ids, occ, domain, osv):
    smem = pl.BlockSpec(memory_space=pltpu.SMEM)
    vmem = pl.BlockSpec(memory_space=pltpu.VMEM)
    return pl.pallas_call(
        tables_kernel,
        in_specs=[smem, smem, smem, smem, vmem, vmem],
        out_specs=vmem,
        out_shape=jax.ShapeDtypeStruct((OCC, TAIL, NOSV), BF16),
        scratch_shapes=[pltpu.VMEM((8, NOSV), I32), pltpu.VMEM((TAIL, NOSV), F32)],
        compiler_params=params(),
        name="slot_tables",
    )(where_am_i, counts, ids, occ, domain, osv)


def fit_kernel(where_am_i, counts, received, metric, tail, fitted, block, acc, whole, sems):
    sub = lax.broadcasted_iota(I32, (CAP, NOSV), 0)
    starts = [jnp.int32(0)] * OCC
    for a in range(NAUX_DEV):
        for k in range(OCC):
            at = pl.multiple_of(jnp.minimum(starts[k] // CAP, CHUNKS - 1) * CAP, CAP)
            here = sub >= starts[k] % CAP
            rows = received[a, k].astype(F32)
            pltpu.store(acc.at[k, pl.ds(at, CAP), :], rows, mask=here)
            pltpu.store(acc.at[k, pl.ds(at + CAP, CAP), :], rows, mask=jnp.logical_not(here))
            starts[k] += counts[a, where_am_i[0] * OCC + k]
    saves = [pltpu.make_async_copy(whole.at[k], block.at[k], sems.at[k]) for k in range(OCC)]
    for k in range(OCC):
        whole[k] = acc[k, :NFIT, :].astype(BF16)
        saves[k].start()
        fitted[k, :NFIT] = jnp.dot(metric[k], whole[k], preferred_element_type=F32).astype(BF16)
        fitted[k, NFIT:] = tail[k]
    for save in saves:
        save.wait()


def fit(where_am_i, counts, received, metric, tail):
    smem = pl.BlockSpec(memory_space=pltpu.SMEM)
    vmem = pl.BlockSpec(memory_space=pltpu.VMEM)
    return pl.pallas_call(
        fit_kernel,
        in_specs=[smem, smem, vmem, vmem, vmem],
        out_specs=[vmem, pl.BlockSpec(memory_space=pltpu.HBM)],
        out_shape=[jax.ShapeDtypeStruct((OCC, ROWS, NOSV), BF16), pltpu.HBM((OCC, NFIT, NOSV), BF16)],
        scratch_shapes=[
            pltpu.VMEM((OCC, NFIT + CAP, NOSV), F32),
            pltpu.VMEM((OCC, NFIT, NOSV), BF16),
            pltpu.SemaphoreType.DMA((OCC,)),
        ],
        compiler_params=params(),
        name="fit",
    )(where_am_i, counts, received, metric, tail)


def spread_rows(source, tail, starts, at_slot, slots, store):
    sub = lax.broadcasted_iota(I32, (AUXD, 2 * CAP), 0).astype(F32)
    lane = lax.broadcasted_iota(I32, (1, 2 * CAP), 1)
    table = tail[0:8, :]
    turned = pltpu.roll(table, CAP, 1)
    lower = lax.broadcasted_iota(I32, (8, 2 * CAP), 1) < CAP
    tables = (jnp.where(lower, table, turned), jnp.where(lower, turned, table))
    for a in range(NAUX_DEV):
        at = pl.multiple_of(starts[at_slot, a], CAP)
        behind = starts[slots + at_slot, a]
        row = tables[a // 8][a % 8 : a % 8 + 1, :]
        row = jnp.where((lane >= behind) & (lane < behind + CAP), row, -1.0)
        pick = jnp.where(sub == row, 1.0, 0.0).astype(BF16)
        store(a, jnp.dot(pick, source[pl.ds(at, 2 * CAP), :], preferred_element_type=F32))


def energy_of(tail):
    return tail[10:11, :] + tail[11:12, :] + tail[12:13, :]


def read_starts(sources, starts_v, starts_s, sem):
    for i, source in enumerate(sources):
        tail = source[NFIT:, :].astype(F32)
        starts_v[i : i + 1, :] = tail[8:9, :].astype(I32)
        starts_v[len(sources) + i : len(sources) + i + 1, :] = tail[9:10, :].astype(I32)
    copy = pltpu.make_async_copy(starts_v, starts_s, sem)
    copy.start()
    copy.wait()


def own_columns(tails):
    rows = [energy_of(t) for t in tails]
    return jnp.concatenate(rows + rows, axis=0).T


def one_round(
    q, slot_of, starts, at_slot, slots, screening, columns, raw_t, spread, ints, amps, energy, density
):
    terms = []
    for l in range(OCC):

        def store(a, value, l=l):
            spread[a * AUXD : (a + 1) * AUXD, l * NOSV : (l + 1) * NOSV] = value.astype(BF16)

        source = slot_of(l)
        tail = source[NFIT:, :].astype(F32)
        terms.append(energy_of(tail))
        spread_rows(source, tail, starts, at_slot + l, slots, store)
    ints[...] = jnp.dot(raw_t[...], spread[...], preferred_element_type=F32)
    for k in range(OCC):
        for l in range(OCC):
            ks = slice(k * NOSV, (k + 1) * NOSV)
            ls = slice(l * NOSV, (l + 1) * NOSV)
            value = ints[ks, ls]
            denominator = columns[:, k : k + 1] + terms[l]
            amp = (screening[k, q, l].astype(F32) * value / denominator).astype(BF16)
            amps[ks, ls] = amp
            part = jnp.sum(amp.astype(F32) * value, axis=0, keepdims=True)
            energy[q, k * OCC + l : k * OCC + l + 1, :] = part

    def add_to(before, after):
        for m in range(NAUX // TILE):
            ms = slice(m * TILE, (m + 1) * TILE)
            value = lax.dot_general(
                spread[ms, :], amps[...], (((1,), (1,)), ((), ())), preferred_element_type=F32
            )
            after[ms, :] = value if before is None else before[ms, :] + value

    density(add_to)


def own_kernel(
    screening, fitted, block_in, raw_out, den, energy,
    block, starts_v, starts_s, spread, ints, amps, sem,
):
    load = pltpu.make_async_copy(block_in, block, sem.at[1])
    load.start()
    read_starts([fitted.at[k] for k in range(OCC)], starts_v, starts_s, sem.at[0])
    load.wait()
    for k in range(OCC):

        def store(a, value, k=k):
            raw_out[k * NOSV : (k + 1) * NOSV, a * AUXD : (a + 1) * AUXD] = value.T.astype(BF16)

        spread_rows(block.at[k], fitted[k, NFIT:, :].astype(F32), starts_s, k, OCC, store)
    energy[...] = jnp.zeros(energy.shape, F32)
    columns = own_columns([fitted[k, NFIT:, :].astype(F32) for k in range(OCC)])

    one_round(
        0, lambda l: fitted.at[l], starts_s, 0, OCC, screening, columns, raw_out, spread, ints, amps, energy,
        lambda add_to: add_to(None, den),
    )


def round_scratch():
    return [
        pltpu.VMEM((NAUX, SLAB), BF16),
        pltpu.VMEM((SLAB, SLAB), F32),
        pltpu.VMEM((SLAB, SLAB), BF16),
    ]


def own_round(screening, fitted, block):
    smem = pl.BlockSpec(memory_space=pltpu.SMEM)
    vmem = pl.BlockSpec(memory_space=pltpu.VMEM)
    return pl.pallas_call(
        own_kernel,
        in_specs=[smem, vmem, pl.BlockSpec(memory_space=pltpu.HBM)],
        out_specs=[vmem, vmem, vmem],
        out_shape=[
            jax.ShapeDtypeStruct((SLAB, NAUX), BF16),
            pltpu.VMEM((NAUX, SLAB), F32),
            jax.ShapeDtypeStruct((5, 16, NOSV), F32),
        ],
        scratch_shapes=[
            pltpu.VMEM(block.shape, BF16),
            pltpu.VMEM((8, NOSV), I32),
            pltpu.SMEM((8, NOSV), I32),
        ]
        + round_scratch()
        + [pltpu.SemaphoreType.DMA((2,))],
        compiler_params=params(),
        name="own_round",
    )(screening, fitted, pltpu.with_memory_space_constraint(block, pltpu.HBM))


def phase_kernel(masks, last, pieces, matchings, screening, own_tail, raw_t, den_in, *rest):
    far = rest[: len(pieces)]
    rest = rest[len(pieces) :]
    if last:
        energy, den_out, source, starts_v, starts_s, spread, ints, amps, piece_sems, sem, den, short, sems = rest
    else:
        den, energy, source, starts_v, starts_s, spread, ints, amps, piece_sems, sem = rest

    def wanted(mask):
        found = mask == masks[0]
        for other in masks[1:]:
            found |= mask == other
        return found

    count = wanted(matchings[0, 0]).astype(I32)
    for q in range(1, 4):
        count += wanted(matchings[q, 0]).astype(I32)
    energy[...] = jnp.zeros(energy.shape, F32)

    def fetch(index):
        mask, lo, hi = pieces[index]
        target = source.at[masks.index(mask), pl.ds(lo, hi - lo)]
        return pltpu.make_async_copy(far[index], target, piece_sems.at[index])

    def send(final):
        tiles = NAUX // TILE
        each = NAUX_DEV // tiles
        sends = []
        for m in range(tiles):
            for a in range(m * each, (m + 1) * each):
                for k in range(OCC):
                    part = final[a * AUXD : (a + 1) * AUXD, k * NOSV : (k + 1) * NOSV]
                    short[a, k] = part.astype(BF16)
            owners = pl.ds(m * each, each)
            copy = pltpu.make_async_copy(short.at[owners], den_out.at[owners], sems.at[m])
            copy.start()
            sends.append(copy)
        for copy in sends:
            copy.wait()

    @pl.when(count > 0)
    def _():
        for index in range(len(pieces)):
            fetch(index).start()
        for index in range(len(pieces)):
            fetch(index).wait()
        slots = [source.at[i, l] for i in range(len(masks)) for l in range(OCC)]
        read_starts(slots, starts_v, starts_s, sem.at[0])
        columns = own_columns([own_tail[k].astype(F32) for k in range(OCC)])

        def body(q, done):
            mask = matchings[q, 0]

            def density(add_to):
                @pl.when(done == 0)
                def _():
                    add_to(den_in, den)

                @pl.when(done > 0)
                def _():
                    add_to(den, den)

            @pl.when(wanted(mask))
            def _():
                which = jnp.int32(0)
                for i in range(1, len(masks)):
                    which = jnp.where(mask == masks[i], i, which)
                one_round(
                    q + 1, lambda l: source.at[which, l], starts_s, which * OCC, len(masks) * OCC, screening, columns,
                    raw_t, spread, ints, amps, energy, density,
                )

            return done + wanted(mask).astype(I32)

        lax.fori_loop(0, 4, body, jnp.int32(0))
        if last:
            send(den)

    @pl.when(count == 0)
    def _():
        if last:
            send(den_in)
        else:
            den[...] = den_in[...]


def phase(masks, last, pieces, matchings, screening, own_tail, raw_t, den, far):
    smem = pl.BlockSpec(memory_space=pltpu.SMEM)
    vmem = pl.BlockSpec(memory_space=pltpu.VMEM)
    hbm = pl.BlockSpec(memory_space=pl.ANY)
    energy = jax.ShapeDtypeStruct((5, 16, NOSV), F32)
    if last:
        sent = (NAUX_DEV, OCC, AUXD, NOSV)
        out_specs = [vmem, hbm]
        out_shape = [energy, pltpu.HBM(sent, BF16)]
        more = [
            pltpu.VMEM((NAUX, SLAB), F32),
            pltpu.VMEM(sent, BF16),
            pltpu.SemaphoreType.DMA((NAUX // TILE,)),
        ]
        alias = {}
    else:
        out_specs = [vmem, vmem]
        out_shape = [pltpu.VMEM((NAUX, SLAB), F32), energy]
        more = []
        alias = {4: 0}
    rows = 2 * len(masks) * OCC
    return pl.pallas_call(
        functools.partial(phase_kernel, masks, last, pieces),
        in_specs=[smem, smem, vmem, vmem, vmem] + [hbm] * len(far),
        out_specs=out_specs,
        out_shape=out_shape,
        scratch_shapes=[
            pltpu.VMEM((len(masks), OCC, ROWS, NOSV), BF16),
            pltpu.VMEM((rows, NOSV), I32),
            pltpu.SMEM((rows, NOSV), I32),
        ]
        + round_scratch()
        + [pltpu.SemaphoreType.DMA((len(pieces),)), pltpu.SemaphoreType.DMA((1,))]
        + more,
        input_output_aliases=alias,
        compiler_params=params(),
        name="phase_" + "_".join(str(m) for m in masks),
    )(matchings, screening, own_tail, raw_t, pltpu.with_memory_space_constraint(den, pltpu.VMEM), *far)


def widen_kernel(short, out, wide, sems):
    part = short.shape[0] // WIDEN_PARTS
    saves = []
    for i in range(WIDEN_PARTS):
        span = pl.ds(i * part, part)
        wide[span] = short[span].astype(F32)
        save = pltpu.make_async_copy(wide.at[span], out.at[span], sems.at[i])
        save.start()
        saves.append(save)
    for save in saves:
        save.wait()


def widen(short):
    return pl.pallas_call(
        widen_kernel,
        in_specs=[pl.BlockSpec(memory_space=pltpu.VMEM)],
        out_specs=pl.BlockSpec(memory_space=pltpu.HBM),
        out_shape=pltpu.HBM(short.shape, F32),
        scratch_shapes=[pltpu.VMEM(short.shape, F32), pltpu.SemaphoreType.DMA((WIDEN_PARTS,))],
        compiler_params=params(),
        name="widen",
    )(short)


def flip(x, mask):
    return lax.ppermute(x, "orb", [(i, i ^ mask) for i in range(lax.axis_size("orb"))])


def per_device(
    raw_rows, fit_metric, domain, counts, orbital_ids, occ_energy, osv_energy, matchings, screening
):
    where_am_i = lax.axis_index("aux").astype(I32).reshape(1)
    group = raw_rows.shape[0]
    counts = counts.T
    packed = pack_rows(where_am_i, domain, counts, raw_rows)
    packed = packed.reshape(NAUX_DEV, OCC, CAP, NOSV)
    received = lax.all_to_all(packed, "aux", split_axis=0, concat_axis=0, tiled=True)
    tail = slot_tables(where_am_i, counts, orbital_ids, occ_energy, domain, osv_energy)
    fitted, block = fit(where_am_i, counts, received, fit_metric, tail)

    near = (flip(fitted, 1), flip(fitted, 2), flip(fitted, 6))
    raw_t, den, energy0 = own_round(screening, fitted, block)
    near, den = lax.optimization_barrier((near, den))
    far1, far2, far6 = near
    middle = (flip(far2, 1), flip(far6, 2), flip(far1, 6))
    common = (matchings, screening, tail, raw_t)
    den, energy1 = phase((1, 2, 6), False, ((1, 0, 4), (2, 0, 4), (6, 0, 4)), *common, den, near)
    middle, den = lax.optimization_barrier((middle, den))
    far3, far4, far7 = middle
    far5 = (flip(far4[0:1], 1), flip(far7[1:2], 2), flip(far3[2:4], 6))
    den, energy2 = phase((3, 4, 7), False, ((3, 0, 4), (4, 0, 4), (7, 0, 4)), *common, den, middle)
    energy3, sent = phase((5,), True, ((5, 0, 1), (5, 1, 2), (5, 2, 4)), *common, den, far5)
    returned = lax.all_to_all(sent, "aux", split_axis=0, concat_axis=0, tiled=True)
    density = widen(returned.reshape(group, AUXD, NOSV))
    total = jnp.sum(energy0 + energy1 + energy2 + energy3, axis=2)
    energies = total.reshape(5, OCC, OCC).transpose(1, 0, 2) * (PAIR_SCALE / (NOSV * NOSV))
    return density, energies


def solution(mesh):
    placed = (
        P("orb", "aux", None),
        P(("orb", "aux"), None, None),
        P("orb", None),
        P("orb", None),
        P(("orb", "aux")),
        P(),
        P(("orb", "aux"), None),
        P(),
        P(("orb", "aux"), None, None),
    )
    return jax.shard_map(
        per_device,
        mesh=mesh,
        in_specs=placed,
        out_specs=(P("orb", "aux", None), P(("orb", "aux"), None, None)),
        check_vma=False,
    )
```
